32 devices in a mesh: grp: 4 (over y, core), dev: 8 (over z, x).
Axes of the slice: x: 2, y: 2, z: 4, core: 2. Of those that a mesh axis runs over, the one named last changes fastest.
Arguments:
- coords: float32 [3, 32768], P(None, ('grp', 'dev')), may hold values from 0 to 6
- counts: int32 [256], P(('grp', 'dev')), may hold values from 64 to 128
- neighbours: int32 [8, 256], P(None, ('grp', 'dev')), may hold values from 0 to 255, as said below
- proxies: float32 [3, 32768], P(None, ('grp', 'dev')), may hold values from -1 to 7
- leaf_transfers: float32 [256, 128, 128], P(('grp', 'dev')), may hold values from -0.375 to 0.375
- node_transfers: float32 [256, 128, 128], P(('grp', 'dev')), may hold values from -0.375 to 0.375
Outputs:
- near_tiles: bfloat16 [256, 8, 128, 128], P(('grp', 'dev'))
- leaf_bases: bfloat16 [32768, 128], P(('grp', 'dev'))
- leaf_factors: float32 [256, 128, 128], P(('grp', 'dev'))
- node_factors: float32 [256, 128, 128], P(('grp', 'dev'))
The draws below stay inside these ranges and needn't reach their ends.
Inputs may be any that keep to these rules, and one draw needn't show every extreme that they name: `neighbours`: row 0 of column l is l itself; every entry of column l differs from l by at most 8.
All inputs are finite; a program needn't handle non-finite values.
Results may differ from the reference program's by a relative error of at most 0.001.
Values sent between devices are 32-bit elements; how exact they have to be, the bound alone decides.
No kernel may reach another device: no remote copies, remote signals or barrier semaphores. Data moves between devices by JAX's collectives and lax.ppermute only.
A program may use at most 64 MiB of HBM per device.

```python
import jax
import jax.numpy as jnp
from jax import lax

LEAF = 128
RANK = 128
NNB = 8
LEAF_DEV = 8
NLEAF = 256
NPTS = 32768


slab_width = 0.02


def draw_coords(key, part):
    uniform_values = jax.random.uniform(key, (3, NPTS), jnp.float32)
    leaf_pos = (jnp.arange(NPTS, dtype=jnp.int32) // LEAF).astype(jnp.float32)
    first = (leaf_pos + uniform_values[0]) * slab_width
    side = uniform_values[1:]
    return jnp.concatenate([first[None, :], side], axis=0)


def draw_proxies(key, part):
    uniform_values = jax.random.uniform(key, (3, NLEAF * RANK), jnp.float32)
    leaf_pos = (jnp.arange(NLEAF * RANK, dtype=jnp.int32) // RANK).astype(jnp.float32)
    first = (leaf_pos + 0.5 + 8.0 * uniform_values[0] - 4.0) * slab_width
    side = 1.5 * uniform_values[1:] - 0.25
    return jnp.concatenate([first[None, :], side], axis=0)


def draw_neighbours(key, part):
    offsets = jax.random.randint(key, (NNB, NLEAF), -LEAF_DEV, LEAF_DEV + 1, dtype=jnp.int32)
    leaf_ids = jnp.arange(NLEAF, dtype=jnp.int32)
    farthest = LEAF_DEV * (1 - 2 * (leaf_ids % 2))
    offsets = offsets.at[0].set(jnp.zeros((NLEAF,), jnp.int32)).at[1].set(farthest)
    return jnp.clip(leaf_ids[None, :] + offsets, 0, NLEAF - 1).astype(jnp.int32)


def plant(values, own_key, smallest, top_value):
    dims = values.shape
    place = [jax.random.randint(jax.random.fold_in(own_key, axis), (), 0, dims[axis]) for axis in range(len(dims))]
    values = values.at[tuple(place)].set(smallest)
    longest = dims.index(max(dims))
    place[longest] = (place[longest] + 1) % dims[longest]
    return values.at[tuple(place)].set(top_value)


def level_of(stream_key, extent, pieces, least, top_value):
    def one(dim, shards_of):
        draws = jax.random.uniform(jax.random.fold_in(jax.random.fold_in(stream_key, 6), dim), (shards_of,), jnp.float32, least / len(pieces), top_value / len(pieces))
        return jnp.repeat(jnp.exp(draws), extent[dim] // shards_of).reshape((-1,) + (1,) * (len(extent) - dim - 1))

    level = one(*pieces[0])
    for cut in pieces[1:]:
        level = level * one(*cut)
    return level


def bell_draw(stream_key, shape, spread, reach, pieces=(), kind=jnp.bfloat16):
    entries = spread * jax.random.normal(stream_key, shape, jnp.float32)
    if pieces:
        entries = entries * level_of(stream_key, shape, pieces, -0.22, 0.18)
    return jnp.clip(entries, -reach, reach).astype(kind)


def setup_inputs(seed: int = 0) -> dict:
    splits = jax.random.split(jax.random.key(seed), 7)
    return {
        "coords": draw_coords(jax.random.fold_in(splits[6], 71), 0),
        "counts": plant(jax.random.randint(splits[1], (NLEAF,), LEAF // 2, LEAF + 1), jax.random.fold_in(splits[1], 1), LEAF // 2, LEAF).astype(jnp.int32),
        "neighbours": draw_neighbours(jax.random.fold_in(splits[6], 71), 0),
        "proxies": draw_proxies(jax.random.fold_in(splits[6], 71), 0),
        "leaf_transfers": bell_draw(splits[4], (NLEAF, RANK, RANK), (2 * RANK) ** -0.5, 0.375, ((0, 32),), jnp.float32),
        "node_transfers": bell_draw(splits[5], (NLEAF, RANK, RANK), (2 * RANK) ** -0.5, 0.375, ((0, 32),), jnp.float32),
    }


ridge = 0.1
length_scale = 0.3

def matern(delta_x, delta_y, delta_z):
    distance = jnp.sqrt(delta_x * delta_x + delta_y * delta_y + delta_z * delta_z)
    scaled = 3.0 ** 0.5 / length_scale * distance
    return (1.0 + scaled) * jnp.exp(-scaled)

def lift(transfer, heads):
    inner = jnp.einsum('lba,lbc->lac', transfer, heads, precision=lax.Precision.HIGHEST)
    return jnp.einsum('lac,lcd->lad', inner, transfer, precision=lax.Precision.HIGHEST)

def factor(heads):
    return jnp.swapaxes(jnp.linalg.cholesky(heads), -1, -2)

def reference(coords, counts, neighbours, proxies, leaf_transfers, node_transfers):
    valid = (jnp.arange(LEAF, dtype=jnp.int32)[None, :] < counts[:, None]).astype(jnp.float32)
    sites = coords.reshape(3, NLEAF, LEAF)
    points = proxies.reshape(3, NLEAF, RANK)
    identity = jnp.eye(RANK, dtype=jnp.float32)

    def tiles_of(leaf):
        own = sites[:, leaf]
        near = neighbours[:, leaf]
        other = jnp.take(sites, near, axis=1)
        other_valid = jnp.take(valid, near, axis=0)
        delta = own[:, None, :, None] - other[:, :, None, :]
        values = matern(delta[0], delta[1], delta[2]) * valid[leaf][None, :, None] * other_valid[:, None, :]
        return values.astype(jnp.bfloat16)
    near_tiles = lax.map(tiles_of, jnp.arange(NLEAF, dtype=jnp.int32))

    def basis_of(leaf):
        delta = sites[:, leaf][:, :, None] - points[:, leaf][:, None, :]
        return matern(delta[0], delta[1], delta[2]) * valid[leaf][:, None]
    basis = lax.map(basis_of, jnp.arange(NLEAF, dtype=jnp.int32))
    gram = jnp.einsum('lik,lij->lkj', basis, basis, precision=lax.Precision.HIGHEST) / LEAF + ridge * identity
    lower = jnp.linalg.cholesky(gram)
    leaf_factors = jnp.swapaxes(lower, -1, -2)
    solved = jax.scipy.linalg.solve_triangular(lower, jnp.swapaxes(basis, -1, -2), lower=True)
    leaf_bases = jnp.swapaxes(solved, -1, -2).reshape(NPTS, RANK).astype(jnp.bfloat16)
    node_factors = jnp.zeros((NLEAF, RANK, RANK), jnp.float32)
    weight = lift(leaf_transfers, gram)
    levels = NLEAF.bit_length() - 1
    root_factor = jnp.zeros((RANK, RANK), jnp.float32)
    for level in range(1, levels + 1):
        heads = weight[0::2] + weight[1::2] + ridge * identity
        first = 2 ** (level - 1)
        stride = 2 ** level
        made = factor(heads)
        node_factors = node_factors.at[first::stride].set(made)
        root_factor = made[0]
        weight = lift(node_transfers[first::stride], heads)
    node_factors = node_factors.at[0].set(root_factor)
    return (near_tiles, leaf_bases, leaf_factors, node_factors)
```

```python
import functools
import math

import jax
import jax.numpy as jnp
from jax import lax
from jax.experimental import pallas as pl
from jax.experimental.pallas import tpu as pltpu
from jax.sharding import PartitionSpec as P

ridge = 0.1
length_scale = 0.3
far = 1.0e6
f32 = jnp.float32
bf16 = jnp.bfloat16
BLOCK = 32
STEP = 4
params = pltpu.CompilerParams(vmem_limit_bytes=48 * 1024 * 1024)


def dot(left, right, left_dim, right_dim):
    return lax.dot_general(
        left,
        right,
        (((left_dim,), (right_dim,)), ((), ())),
        precision=lax.Precision.HIGHEST,
        preferred_element_type=f32,
    )


def matern(delta_x, delta_y, delta_z):
    scale = 3.0**0.5 / length_scale * math.log2(math.e)
    square = delta_x * delta_x + delta_y * delta_y + delta_z * delta_z
    square = jnp.maximum(square * (scale * scale), 1e-30)
    u = square * lax.rsqrt(square)
    return (1.0 + u * math.log(2.0)) * jnp.exp2(-u)


def lane_copies(vreg, lane):
    return jnp.broadcast_to(vreg[:, lane : lane + 1], vreg.shape)


def row_copies(vreg, row):
    return jnp.broadcast_to(vreg[row : row + 1, :], vreg.shape)


def eliminate(block, extra, base, step):
    batch = len(block)
    groups = len(block[0])
    count = 8 * groups
    rows = [[None] * count for _ in range(batch)]
    extra_rows = [[None] * count for _ in range(batch)]
    for j in range(0, count, step):
        g, s = divmod(j, 8)
        for b in range(batch):
            own = block[b]
            cols = [[lane_copies(own[q], base + j + k) for k in range(step)] for q in range(g, groups)]
            width = 2 if extra else 1
            rho = [
                [row_copies(side[b][g], s + k) for k in range(step)]
                for side in ((block, extra) if extra else (block,))
            ]
            pivot = [[row_copies(cols[0][k], s + i) for k in range(i + 1)] for i in range(step)]
            low = [[None] * step for _ in range(step)]
            inv = [None] * step
            made = [[None] * step for _ in range(width)]
            for i in range(step):
                for k in range(i):
                    t = pivot[i][k]
                    for m in range(k):
                        t = t - low[i][m] * low[k][m]
                    low[i][k] = t * inv[k]
                t = pivot[i][i]
                for m in range(i):
                    t = t - low[i][m] * low[i][m]
                inv[i] = lax.rsqrt(t)
                for side in range(width):
                    u = rho[side][i]
                    for m in range(i):
                        u = u - low[i][m] * made[side][m]
                    made[side][i] = u * inv[i]
            for k in range(step):
                rows[b][j + k] = made[0][k]
                if extra:
                    extra_rows[b][j + k] = made[1][k]
            if j + step == count:
                continue
            for side in range(width):
                back = [None] * step
                for i in reversed(range(step)):
                    t = made[side][i]
                    for m in range(i + 1, step):
                        t = t - low[m][i] * back[m]
                    back[i] = t * inv[i]
                target = (block, extra)[side][b]
                for q in range(g, groups):
                    if q == g and s + step >= 8:
                        continue
                    t = target[q]
                    for k in range(step):
                        t = t - cols[q - g][k] * back[k]
                    target[q] = t
    return rows, extra_rows


def gather_rows(rows, row_id):
    value = rows[0]
    for i in range(1, 8):
        value = jnp.where(row_id == i, rows[i], value)
    return value


def factor_block(load, store, batch, k, extra):
    row_id = lax.broadcasted_iota(jnp.int32, (8, 128), 0)
    lane_id = lax.broadcasted_iota(jnp.int32, (8, 128), 1)
    block = []
    for b in range(batch):
        value = load(b)
        block.append([value[8 * q : 8 * q + 8, :] for q in range(BLOCK // 8)])
    start = []
    if extra:
        unit = [jnp.where(lane_id == row_id + 8 * q, 1.0, 0.0).astype(f32) for q in range(BLOCK // 8)]
        start = [list(unit) for _ in range(batch)]
    rows, extra_rows = eliminate(block, start, k * BLOCK, STEP)
    inverses = []
    for b in range(batch):
        pieces = []
        for q in range(BLOCK // 8):
            at = k * BLOCK + 8 * q
            value = gather_rows(rows[b][8 * q : 8 * q + 8], row_id)
            store(b, at, jnp.where(lane_id >= row_id + at, value, 0.0))
            if extra:
                pieces.append(gather_rows(extra_rows[b][8 * q : 8 * q + 8], row_id))
        if extra:
            inverses.append(jnp.concatenate(pieces, axis=0)[:, :BLOCK])
    return inverses


def panel(matrix, factor_ref, slot, k):
    at = k * BLOCK
    value = matrix[at : at + BLOCK, :]
    if k:
        done = factor_ref[slot, 0:at, :]
        value = value - dot(done[:, at : at + BLOCK], done, 0, 0)
    return value


def local_kernel(counts, coords, proxies, leaf_t, node_t, basis_ref, gram_ref, heads_ref, weight_ref):
    leaves = basis_ref.shape[0]
    eye = jnp.where(
        lax.broadcasted_iota(jnp.int32, (128, 128), 0) == lax.broadcasted_iota(jnp.int32, (128, 128), 1),
        ridge,
        0.0,
    ).astype(f32)
    lane_id = lax.broadcasted_iota(jnp.int32, (1, 128), 1)
    weights = []
    for leaf in range(leaves):
        span = slice(leaf * 128, leaf * 128 + 128)
        own = jnp.concatenate(
            [
                jnp.where(lane_id < counts[leaf], coords[0:1, span], far),
                coords[1:3, span],
                jnp.zeros((5, 128), f32),
            ],
            axis=0,
        )
        own = own.T
        basis = matern(
            own[:, 0:1] - proxies[0:1, span],
            own[:, 1:2] - proxies[1:2, span],
            own[:, 2:3] - proxies[2:3, span],
        )
        basis_ref[leaf] = basis
        gram = dot(basis, basis, 0, 0) * (1.0 / 128) + eye
        gram_ref[leaf] = gram
        move = leaf_t[leaf]
        weights.append(dot(move, dot(gram, move, 1, 0), 0, 0))
    at = 0
    level = 1
    while len(weights) > 1:
        following = []
        for k in range(len(weights) // 2):
            head = weights[2 * k] + weights[2 * k + 1] + eye
            heads_ref[at] = head
            at += 1
            move = node_t[k * 2**level + 2 ** (level - 1)]
            following.append(dot(move, dot(head, move, 1, 0), 0, 0))
        weights = following
        level += 1
    weight_ref[...] = weights[0]


def lift_kernel(low_ref, high_ref, move_ref, head_ref, weight_ref):
    eye = jnp.where(
        lax.broadcasted_iota(jnp.int32, (128, 128), 0) == lax.broadcasted_iota(jnp.int32, (128, 128), 1),
        ridge,
        0.0,
    ).astype(f32)
    head = low_ref[...] + high_ref[...] + eye
    head_ref[...] = head
    move = move_ref[...]
    weight_ref[...] = dot(move, dot(head, move, 1, 0), 0, 0)


def near_kernel(ids, counts, own_ref, low_ref, high_ref, out_ref, wide):
    leaves = counts.shape[0]
    span = own_ref.shape[1]
    fan = ids.shape[0]
    wide[:, 0:span] = low_ref[...]
    wide[:, span : 2 * span] = own_ref[...]
    wide[:, 2 * span : 3 * span] = high_ref[...]
    lane_id = lax.broadcasted_iota(jnp.int32, (1, 128), 1)

    def leaf_step(leaf, carry):
        start = pl.multiple_of(leaf * 128, 128)
        own = own_ref[:, pl.ds(start, 128)]
        own = jnp.concatenate(
            [jnp.where(lane_id < counts[leaf], own[0:1], far), own[1:3], jnp.zeros((5, 128), f32)], axis=0
        )
        own = own.T
        own_x = jnp.broadcast_to(own[:, 0:1], (128, 128))
        own_y = jnp.broadcast_to(own[:, 1:2], (128, 128))
        own_z = jnp.broadcast_to(own[:, 2:3], (128, 128))
        for n in range(fan):
            at = pl.multiple_of(ids[n, leaf] * 128, 128)
            other = wide[:, pl.ds(at, 128)]
            tile = matern(own_x - other[0:1], own_y - other[1:2], own_z - other[2:3])
            out_ref[leaf, n] = tile.astype(bf16)
        return carry

    lax.fori_loop(0, leaves, leaf_step, 0)


def leaf_kernel(basis_ref, gram_ref, factor_ref, bases_ref, x_ref):
    batch = gram_ref.shape[0]

    def store(b, at, value):
        factor_ref[b, at : at + 8, :] = value

    for k in range(128 // BLOCK):
        at = k * BLOCK
        inverses = factor_block(lambda b: panel(gram_ref[b], factor_ref, b, k), store, batch, k, True)
        for b in range(batch):
            value = basis_ref[b, :, at : at + BLOCK]
            if k:
                value = value - dot(x_ref[b, :, 0:at], factor_ref[b, 0:at, at : at + BLOCK], 1, 0)
            x_ref[b, :, at : at + BLOCK] = dot(value, inverses[b], 1, 1)
    for b in range(batch):
        bases_ref[b * 128 : b * 128 + 128, :] = x_ref[b].astype(bf16)


def node_kernel(heads_ref, top_ref, factor_ref):
    inner = heads_ref.shape[0]
    batch = inner + 1
    slots = []
    level = 1
    while 2**level <= batch:
        slots += [k * 2**level + 2 ** (level - 1) for k in range(batch // 2**level)]
        level += 1
    slots.append(0)

    def matrix(b):
        return heads_ref[b] if b < inner else top_ref[...]

    def store(b, at, value):
        factor_ref[slots[b], at : at + 8, :] = value

    for k in range(128 // BLOCK):
        factor_block(lambda b: panel(matrix(b), factor_ref, slots[b], k), store, batch, k, False)


def partner(value, distance):
    count = lax.axis_size("grp") * lax.axis_size("dev")
    return lax.ppermute(value, ("grp", "dev"), [(i, i ^ 1 << distance) for i in range(count)])


def trailing(value, count):
    total = jnp.zeros((), jnp.int32)
    for bit in range(1, count + 1):
        total = total + (value % (1 << bit) == 0).astype(jnp.int32)
    return total


vmem = pl.BlockSpec(memory_space=pltpu.VMEM)
smem = pl.BlockSpec(memory_space=pltpu.SMEM)


def shards(coords, counts, neighbours, proxies, leaf_transfers, node_transfers):
    leaves = counts.shape[0]
    slots = coords.shape[1] // leaves
    width = leaf_transfers.shape[1]
    fan = neighbours.shape[0]
    count = lax.axis_size("grp") * lax.axis_size("dev")
    position = lax.axis_index("grp") * lax.axis_size("dev") + lax.axis_index("dev")
    mat = jax.ShapeDtypeStruct((width, width), f32)
    mats = jax.ShapeDtypeStruct((leaves, width, width), f32)

    valid = jnp.arange(slots, dtype=jnp.int32)[None, :] < counts[:, None]
    keep = valid.reshape(1, leaves * slots) | (jnp.arange(3, dtype=jnp.int32)[:, None] > 0)
    masked = jnp.where(keep, coords, -far)
    up = [(i, i + 1) for i in range(count - 1)]
    down = [(target, source) for source, target in up]
    low = lax.ppermute(masked, ("grp", "dev"), up)
    high = lax.ppermute(masked, ("grp", "dev"), down)

    total_levels = count.bit_length() - 1
    owners = []
    first = node_transfers[0]
    for level in range(total_levels - 1):
        other = partner(first, level)
        upper = position // (1 << level) % 2 == 1
        owners.append(jnp.where(upper, first, other))
        first = jnp.where(upper, other, first)

    basis, gram, heads, weight = pl.pallas_call(
        local_kernel,
        out_shape=(mats, mats, jax.ShapeDtypeStruct((leaves - 1, width, width), f32), mat),
        in_specs=[smem, vmem, vmem, vmem, vmem],
        out_specs=(vmem, vmem, vmem, vmem),
        compiler_params=params,
        name="local",
    )(counts, coords, proxies, leaf_transfers, node_transfers)

    lift = pl.pallas_call(
        lift_kernel,
        out_shape=(mat, mat),
        in_specs=[vmem, vmem, vmem],
        out_specs=(vmem, vmem),
        compiler_params=params,
        name="lift",
    )
    identity = ridge * jnp.eye(width, dtype=f32)
    tz_all = trailing(position, total_levels - 1)
    chosen = jnp.zeros((width, width), f32)
    for level in range(total_levels):
        other = partner(weight, level)
        if level + 1 < total_levels:
            head, following = lift(weight, other, owners[level])
        else:
            head = weight + other + identity
        chosen = jnp.where(tz_all == level, head, chosen)
        weight = following

    near_tiles = pl.pallas_call(
        near_kernel,
        out_shape=jax.ShapeDtypeStruct((leaves, fan, slots, slots), bf16),
        in_specs=[smem, smem, vmem, vmem, vmem],
        out_specs=vmem,
        scratch_shapes=[pltpu.VMEM((3, 3 * leaves * slots), f32)],
        compiler_params=params,
        name="near",
    )(neighbours - (position * leaves - leaves), counts, masked, low, high)

    leaf_factors, leaf_bases = pl.pallas_call(
        leaf_kernel,
        out_shape=(mats, jax.ShapeDtypeStruct((leaves * slots, width), bf16)),
        in_specs=[vmem, vmem],
        out_specs=(vmem, vmem),
        scratch_shapes=[pltpu.VMEM((leaves, slots, width), f32)],
        compiler_params=params,
        name="leaf",
    )(basis, gram)

    node_factors = pl.pallas_call(
        node_kernel,
        out_shape=mats,
        in_specs=[vmem, vmem],
        out_specs=vmem,
        compiler_params=params,
        name="node",
    )(heads, chosen)
    return (near_tiles, leaf_bases, leaf_factors, node_factors)


def solution(mesh):
    both = ("grp", "dev")
    in_specs = (
        P(None, both),
        P(both),
        P(None, both),
        P(None, both),
        P(both, None, None),
        P(both, None, None),
    )
    out_specs = (
        P(both, None, None, None),
        P(both, None),
        P(both, None, None),
        P(both, None, None),
    )
    return jax.shard_map(shards, mesh=mesh, in_specs=in_specs, out_specs=out_specs, check_vma=False)
```

```python
import functools
import math

import jax
import jax.numpy as jnp
from jax import lax
from jax.experimental import pallas as pl
from jax.experimental.pallas import tpu as pltpu
from jax.sharding import PartitionSpec as P

ridge = 0.1
length_scale = 0.3
far = 1.0e6
f32 = jnp.float32
bf16 = jnp.bfloat16
BLOCK = 32
STEP = 8
WIDTH = 128
GROUP = 8
params = pltpu.CompilerParams(vmem_limit_bytes=40 * 1024 * 1024)
vmem = pl.BlockSpec(memory_space=pltpu.VMEM)
smem = pl.BlockSpec(memory_space=pltpu.SMEM)
anywhere = pl.BlockSpec(memory_space=pltpu.HBM)


def cost(micros):
    return pl.CostEstimate(flops=int(micros * 1.0e9), bytes_accessed=int(micros * 3.0e6), transcendentals=0)


def iota(shape, dim):
    return lax.broadcasted_iota(jnp.int32, shape, dim)


def split(value):
    high = value.astype(bf16)
    return high, (value - high.astype(f32)).astype(bf16)


def product(left, right, left_dim, right_dim):
    def dot(a, b):
        return lax.dot_general(a, b, (((left_dim,), (right_dim,)), ((), ())), preferred_element_type=f32)

    (lh, ll), (rh, rl) = split(left), split(right)
    return dot(lh, rh) + (dot(lh, rl) + dot(ll, rh))


def lift(move, head):
    return product(move, product(head, move, 1, 0), 0, 0)


def unit(scale):
    shape = (WIDTH, WIDTH)
    return jnp.where(iota(shape, 0) == iota(shape, 1), scale, 0.0).astype(f32)


def matern(delta_x, delta_y, delta_z):
    scale = 3.0**0.5 / length_scale * math.log2(math.e)
    square = delta_x * delta_x + delta_y * delta_y + delta_z * delta_z
    square = jnp.maximum(square * (scale * scale), 1e-30)
    u = square * lax.rsqrt(square)
    return (1.0 + u * math.log(2.0)) * jnp.exp2(-u)


def site_columns(own, count):
    moved = jnp.where(iota((1, WIDTH), 1) < count, own[0:1], far)
    return jnp.concatenate([moved, own[1:3], jnp.zeros((5, WIDTH), f32)], axis=0).T


def lane_copies(vreg, lane):
    return jnp.broadcast_to(vreg[:, lane : lane + 1], vreg.shape)


def add_up(terms):
    while len(terms) > 1:
        terms = [
            terms[a] + terms[a + 1] if a + 1 < len(terms) else terms[a] for a in range(0, len(terms), 2)
        ]
    return terms[0]


def eliminate(rows, base, inverse, store_r, store_s, filler):
    lane = iota((GROUP, WIDTH), 1)
    count = len(rows)
    rows = list(rows)
    for j in range(0, count, STEP):
        at = base + j
        cols = [[lane_copies(rows[i], at + k) for k in range(min(STEP, i - j + 1))] for i in range(j, count)]
        filler(at // STEP)
        spot = (lane >= at) & (lane < at + STEP)
        low = [[None] * STEP for _ in range(STEP)]
        inv = [None] * STEP
        made = [None] * STEP
        made_s = [None] * STEP
        for i in range(STEP):
            for k in range(i):
                t = cols[i][k]
                for m in range(k):
                    t = t - low[i][m] * low[k][m]
                low[i][k] = t * inv[k]
            t = cols[i][i]
            for m in range(i):
                t = t - low[i][m] * low[i][m]
            inv[i] = lax.rsqrt(t)
            u = rows[j + i]
            for m in range(i):
                u = u - low[i][m] * made[m]
            made[i] = u * inv[i]
            store_r(at + i, made[i])
            if inverse:
                u = jnp.where(spot, jnp.where(lane == at + i, 1.0, 0.0).astype(f32), rows[j + i])
                for m in range(i):
                    u = u - low[i][m] * made_s[m]
                made_s[i] = u * inv[i]
                store_s(at + i, made_s[i])
        if j + STEP >= count:
            break
        source = made_s if inverse else made
        back = [None] * STEP
        for i in reversed(range(STEP)):
            t = source[i]
            for m in range(i + 1, STEP):
                t = t - low[m][i] * back[m]
            back[i] = t * inv[i]
        for i in range(j + STEP, count):
            t = jnp.where(spot, 0.0, rows[i]) if inverse else rows[i]
            rows[i] = t - add_up([cols[i - j][k] * back[k] for k in range(STEP)])


def stacked(ref, matrix, first, count):
    return ref[pl.ds(GROUP * first + matrix, count, stride=GROUP), :]


def factor_block(k, load, r_refs, s_refs, store_r, store_s, update, filler):
    base = k * BLOCK
    inverse = s_refs is not None
    if k:
        for b in range(GROUP):
            total = None
            for m in range(k):
                r = stacked(r_refs[m], b, 0, BLOCK)
                right = r
                if inverse:
                    lane = iota((BLOCK, WIDTH), 1)
                    row = iota((BLOCK, WIDTH), 0) + m * BLOCK
                    right = jnp.where(lane >= base, r, 0.0)
                    right = jnp.where(lane <= row, stacked(s_refs[m], b, 0, BLOCK), right)
                pieces = (r[:, base : base + BLOCK], right)
                total = (
                    pieces
                    if total is None
                    else tuple(jnp.concatenate([t, p], axis=0) for t, p in zip(total, pieces))
                )
            update[pl.ds(b, BLOCK, stride=GROUP), :] = product(total[0], total[1], 0, 0)
    lane = iota((GROUP, WIDTH), 1)
    rows = []
    for i in range(BLOCK):
        t = load(base + i)
        if k:
            if inverse:
                t = jnp.where(lane >= base, t, 0.0)
            t = t - update[GROUP * i : GROUP * (i + 1), :]
        rows.append(t)
    eliminate(rows, base, inverse, store_r, store_s, filler)


def write_factor(b, r_refs, target):
    for m, r_ref in enumerate(r_refs):
        shape = (BLOCK, WIDTH)
        keep = iota(shape, 1) >= iota(shape, 0) + m * BLOCK
        target[m * BLOCK : (m + 1) * BLOCK, :] = jnp.where(keep, stacked(r_ref, b, 0, BLOCK), 0.0)


def position():
    return lax.axis_index("grp") * lax.axis_size("dev") + lax.axis_index("dev")


def local_kernel(
    counts_in, coords_in, proxies_in, leaf_in, node_in,
    basis_ref, gram_ref, heads_ref, weight_ref, move_ref,
    counts, coords, proxies, leaf_t, node_t, sems,
):
    pairs = ((counts_in, counts), (coords_in, coords), (proxies_in, proxies), (leaf_in, leaf_t), (node_in, node_t))
    copies = [pltpu.make_async_copy(a, b, sems.at[i]) for i, (a, b) in enumerate(pairs)]
    for copy in copies:
        copy.start()
    leaves = basis_ref.shape[0]
    eye = unit(ridge)
    for copy in copies[:3]:
        copy.wait()
    grams = []
    for leaf in range(leaves):
        span = slice(leaf * WIDTH, leaf * WIDTH + WIDTH)
        own = site_columns(coords[:, span], counts[leaf])
        basis = matern(
            own[:, 0:1] - proxies[0:1, span],
            own[:, 1:2] - proxies[1:2, span],
            own[:, 2:3] - proxies[2:3, span],
        )
        basis_ref[leaf] = basis
        gram = product(basis, basis, 0, 0) * (1.0 / WIDTH) + eye
        gram_ref[pl.ds(leaf, WIDTH, stride=GROUP), :] = gram
        grams.append(gram)
    copies[3].wait()
    weights = [lift(leaf_t[leaf], grams[leaf]) for leaf in range(leaves)]
    copies[4].wait()
    move_ref[...] = node_t[0]
    at = 0
    level = 1
    while len(weights) > 1:
        following = []
        for k in range(len(weights) // 2):
            head = weights[2 * k] + weights[2 * k + 1] + eye
            heads_ref[pl.ds(at, WIDTH, stride=GROUP), :] = head
            at += 1
            following.append(lift(node_t[k * 2**level + 2 ** (level - 1)], head))
        weights = following
        level += 1
    weight_ref[...] = weights[0]


def lift_kernel(left, right, move, chosen_in, weight_ref, chosen_ref, *, level):
    head = left[...] + right[...] + unit(ridge)
    mine = position() % (2 ** (level + 1)) == 2**level
    chosen_ref[...] = jnp.where(mine, head, chosen_in[...])
    weight_ref[...] = lift(move[...], head)


def leaf_kernel(*refs, k, leaves):
    refs = list(refs)
    counts, ids, own_ref, low_ref, high_ref, gram_ref = refs[:6]
    r_done, s_done = refs[6 : 6 + k], refs[6 + k : 6 + 2 * k]
    refs = refs[6 + 2 * k :]
    last = k == WIDTH // BLOCK - 1
    if last:
        basis_ref = refs.pop(0)
    if k:
        refs.pop(0)
    near_out, r_out, s_out = refs[:3]
    refs = refs[3:]
    if last:
        factor_ref, bases_ref = refs[:2]
        refs = refs[2:]
    wide, tiles, update, sems = refs
    span = own_ref.shape[1]
    fan = ids.shape[0]
    share = leaves // (WIDTH // BLOCK)
    wide[:, 0:span] = low_ref[...]
    wide[:, span : 2 * span] = own_ref[...]
    wide[:, 2 * span : 3 * span] = high_ref[...]
    offset = (position() - 1) * leaves
    held = {}

    def tile(t):
        leaf, n = divmod(t, fan)
        at = k * share + leaf
        if n == 0:
            own = site_columns(own_ref[:, at * WIDTH : (at + 1) * WIDTH], counts[at])
            held[leaf] = [jnp.broadcast_to(own[:, d : d + 1], (WIDTH, WIDTH)) for d in range(3)]
        own = held[leaf]
        other = wide[:, pl.ds(pl.multiple_of((ids[n, at] - offset) * WIDTH, WIDTH), WIDTH)]
        value = matern(own[0] - other[0:1], own[1] - other[1:2], own[2] - other[2:3])
        tiles[leaf, n] = value.astype(bf16)
        if n == fan - 1:
            pltpu.make_async_copy(tiles.at[leaf], near_out.at[at], sems.at[leaf]).start()

    each = share * fan // (BLOCK // STEP)

    def filler(step):
        first = (step % (BLOCK // STEP)) * each
        for t in range(first, first + each):
            tile(t)

    def store_r(i, value):
        r_out[GROUP * (i - k * BLOCK) : GROUP * (i - k * BLOCK + 1), :] = value

    def store_s(i, value):
        s_out[GROUP * (i - k * BLOCK) : GROUP * (i - k * BLOCK + 1), :] = value

    def load(i):
        return gram_ref[GROUP * i : GROUP * (i + 1), :]

    factor_block(k, load, r_done, s_done, store_r, store_s, update, filler)
    if last:
        r_all, s_all = list(r_done) + [r_out], list(s_done) + [s_out]
        for b in range(GROUP):
            write_factor(b, r_all, factor_ref.at[b])
            shape = (WIDTH, WIDTH)
            turned = jnp.concatenate([stacked(s, b, 0, BLOCK) for s in s_all], axis=0)
            turned = jnp.where(iota(shape, 1) <= iota(shape, 0), turned, 0.0)
            bases_ref[b * WIDTH : (b + 1) * WIDTH, :] = product(basis_ref[b], turned, 1, 1).astype(bf16)
    for leaf in range(share):
        pltpu.make_async_copy(tiles.at[leaf], near_out.at[k * share + leaf], sems.at[leaf]).wait()


def node_kernel(heads_ref, left, right, chosen, factor_ref, r_ref, update, *, half):
    top_row = jnp.where(position() % half == 0, left[...] + right[...] + unit(ridge), chosen[...])
    group = iota((GROUP, WIDTH), 0)
    blocks = [r_ref.at[pl.ds(m * BLOCK * GROUP, BLOCK * GROUP), :] for m in range(WIDTH // BLOCK)]
    slots = []
    level = 1
    while 2**level <= GROUP:
        slots += [k * 2**level + 2 ** (level - 1) for k in range(GROUP // 2**level)]
        level += 1
    slots.append(0)

    def load(i):
        top = jnp.broadcast_to(top_row[i : i + 1, :], (GROUP, WIDTH))
        return jnp.where(group == GROUP - 1, top, heads_ref[GROUP * i : GROUP * (i + 1), :])

    def store(i, value):
        r_ref[GROUP * i : GROUP * (i + 1), :] = value

    for k in range(WIDTH // BLOCK):
        factor_block(k, load, blocks[:k], None, store, None, update, lambda step: None)
    for b in range(GROUP):
        write_factor(b, blocks, factor_ref.at[slots[b]])


def tied(first, *others):
    return lax.optimization_barrier((first, *others))[0]


def shards(coords, counts, neighbours, proxies, leaf_transfers, node_transfers):
    leaves = counts.shape[0]
    slots = coords.shape[1] // leaves
    fan = neighbours.shape[0]
    count = lax.axis_size("grp") * lax.axis_size("dev")
    levels = count.bit_length() - 1
    half = count // 2
    both = ("grp", "dev")
    mat = jax.ShapeDtypeStruct((WIDTH, WIDTH), f32)
    mats = jax.ShapeDtypeStruct((leaves, WIDTH, WIDTH), f32)
    flat = jax.ShapeDtypeStruct((WIDTH * GROUP, WIDTH), f32)
    part = jax.ShapeDtypeStruct((BLOCK * GROUP, WIDTH), f32)

    valid = jnp.arange(slots, dtype=jnp.int32)[None, :] < counts[:, None]
    keep = valid.reshape(1, leaves * slots) | (jnp.arange(3, dtype=jnp.int32)[:, None] > 0)
    masked = jnp.where(keep, coords, -far)
    up = [(i, i + 1) for i in range(count - 1)]
    low = lax.ppermute(masked, both, up)
    high = lax.ppermute(masked, both, [(target, source) for source, target in up])

    basis, gram, heads, weight, move = pl.pallas_call(
        local_kernel,
        out_shape=(mats, flat, flat, mat, mat),
        in_specs=[anywhere] * 5,
        out_specs=(vmem,) * 5,
        scratch_shapes=[
            pltpu.SMEM(counts.shape, jnp.int32),
            pltpu.VMEM(coords.shape, f32),
            pltpu.VMEM(proxies.shape, f32),
            pltpu.VMEM(leaf_transfers.shape, f32),
            pltpu.VMEM(node_transfers.shape, f32),
            pltpu.SemaphoreType.DMA((5,)),
        ],
        compiler_params=params,
        cost_estimate=cost(4),
        name="local",
    )(*(pltpu.with_memory_space_constraint(x, pltpu.HBM) for x in (counts, coords, proxies, leaf_transfers, node_transfers)))

    chunks = WIDTH // BLOCK
    r_parts, s_parts = [], []
    near = None
    chosen = weight

    def leaf_chunk(k, after):
        nonlocal near
        last = k == chunks - 1
        operands = [counts, neighbours, tied(masked, after), low, high, gram, *r_parts, *s_parts]
        specs = [smem, smem] + [vmem] * (4 + 2 * k)
        if last:
            operands.append(basis)
            specs.append(vmem)
        if k:
            operands.append(near)
            specs.append(anywhere)
        shapes = [jax.ShapeDtypeStruct((leaves, fan, slots, slots), bf16), part, part]
        outs = [anywhere, vmem, vmem]
        if last:
            shapes += [mats, jax.ShapeDtypeStruct((leaves * slots, WIDTH), bf16)]
            outs += [vmem, vmem]
        near, r, s, *rest = pl.pallas_call(
            functools.partial(leaf_kernel, k=k, leaves=leaves),
            out_shape=shapes,
            in_specs=specs,
            out_specs=outs,
            scratch_shapes=[
                pltpu.VMEM((3, 3 * leaves * slots), f32),
                pltpu.VMEM((leaves // chunks, fan, slots, slots), bf16),
                pltpu.VMEM((BLOCK * GROUP, WIDTH), f32),
                pltpu.SemaphoreType.DMA((leaves // chunks,)),
            ],
            input_output_aliases={len(operands) - 1: 0} if k else {},
            compiler_params=params,
            cost_estimate=cost(2.5),
            name=f"leaf{k}",
        )(*operands)
        r_parts.append(r)
        s_parts.append(s)
        return r, rest

    rest = None
    for level in range(levels):
        span = 2 ** (level + 1)
        if level == 0:
            left = lax.ppermute(weight, both, [(i, i + 1) for i in range(0, count, 2)])
            right = weight
        else:
            quarter = span // 4
            first = [(i + quarter, i + 2 * quarter) for i in range(0, count, span)]
            second = [(i + 3 * quarter, i + 2 * quarter) for i in range(0, count, span)]
            if level + 1 == levels:
                first.append((3 * quarter, 0))
                second.append((quarter, 0))
            left = lax.ppermute(weight, both, first)
            right = lax.ppermute(weight, both, second)
        if level < chunks:
            mark, rest = leaf_chunk(level, weight)
            left = tied(left, mark)
        if level + 1 < levels:
            weight, chosen = pl.pallas_call(
                functools.partial(lift_kernel, level=level),
                out_shape=(mat, mat),
                in_specs=[vmem] * 4,
                out_specs=(vmem,) * 2,
                compiler_params=params,
                cost_estimate=cost(0.4),
                name=f"lift{level}",
            )(left, right, move, chosen)
    leaf_factors, leaf_bases = rest

    node_factors = pl.pallas_call(
        functools.partial(node_kernel, half=half),
        out_shape=mats,
        in_specs=[vmem] * 4,
        out_specs=vmem,
        scratch_shapes=[pltpu.VMEM((WIDTH * GROUP, WIDTH), f32), pltpu.VMEM((BLOCK * GROUP, WIDTH), f32)],
        compiler_params=params,
        cost_estimate=cost(6),
        name="node",
    )(heads, left, right, chosen)
    return (near, leaf_bases, leaf_factors, node_factors)


def solution(mesh):
    both = ("grp", "dev")
    in_specs = (
        P(None, both),
        P(both),
        P(None, both),
        P(None, both),
        P(both, None, None),
        P(both, None, None),
    )
    out_specs = (
        P(both, None, None, None),
        P(both, None),
        P(both, None, None),
        P(both, None, None),
    )
    return jax.shard_map(shards, mesh=mesh, in_specs=in_specs, out_specs=out_specs, check_vma=False)
```

```python
import functools
import math

import jax
import jax.numpy as jnp
from jax import lax
from jax.experimental import pallas as pl
from jax.experimental.pallas import tpu as pltpu
from jax.sharding import PartitionSpec as P

ridge = 0.1
length_scale = 0.3
far = 1.0e6
f32 = jnp.float32
bf16 = jnp.bfloat16
STEP = 8
WIDTH = 128
GROUP = 8
STEPS = WIDTH // STEP
params = pltpu.CompilerParams(vmem_limit_bytes=40 * 1024 * 1024)
vmem = pl.BlockSpec(memory_space=pltpu.VMEM)
smem = pl.BlockSpec(memory_space=pltpu.SMEM)
anywhere = pl.BlockSpec(memory_space=pl.ANY)


def cost(micros):
    return pl.CostEstimate(flops=int(micros * 1.0e9), bytes_accessed=int(micros * 3.0e6), transcendentals=0)


def iota(shape, dim):
    return lax.broadcasted_iota(jnp.int32, shape, dim)


def split(value):
    high = value.astype(bf16)
    return high, (value - high.astype(f32)).astype(bf16)


def product(left, right, left_dim, right_dim):
    def dot(a, b):
        return lax.dot_general(a, b, (((left_dim,), (right_dim,)), ((), ())), preferred_element_type=f32)

    (lh, ll), (rh, rl) = split(left), split(right)
    return dot(lh, rh) + (dot(lh, rl) + dot(ll, rh))


def lift(move, head):
    return product(move, product(head, move, 1, 0), 0, 0)


def unit(scale):
    shape = (WIDTH, WIDTH)
    return jnp.where(iota(shape, 0) == iota(shape, 1), scale, 0.0).astype(f32)


def matern(delta_x, delta_y, delta_z):
    scale = 3.0**0.5 / length_scale * math.log2(math.e)
    square = delta_x * delta_x + delta_y * delta_y + delta_z * delta_z
    square = jnp.maximum(square * (scale * scale), 1e-30)
    u = square * lax.rsqrt(square)
    return (1.0 + u * math.log(2.0)) * jnp.exp2(-u)


def lane_copies(vreg, lane):
    return jnp.broadcast_to(vreg[:, lane : lane + 1], vreg.shape)


def add_up(terms):
    while len(terms) > 1:
        terms = [
            terms[a] + terms[a + 1] if a + 1 < len(terms) else terms[a] for a in range(0, len(terms), 2)
        ]
    return terms[0]


def rows_of(ref, i):
    return ref[GROUP * i : GROUP * (i + 1), :]


def stacked(ref, matrix):
    return ref[pl.ds(matrix, ref.shape[0] // GROUP, stride=GROUP), :]


def eliminate(s, get, put, put_r, put_s):
    at = STEP * s
    lane = iota((GROUP, WIDTH), 1)
    pivots = [get(at + i) for i in range(STEP)]
    cols = [[lane_copies(pivots[i], at + k) for k in range(i + 1)] for i in range(STEP)]
    spot = (lane >= at) & (lane < at + STEP)
    low = [[None] * STEP for _ in range(STEP)]
    inv = [None] * STEP
    made = [None] * STEP
    made_s = [None] * STEP
    for i in range(STEP):
        for k in range(i):
            t = cols[i][k]
            for m in range(k):
                t = t - low[i][m] * low[k][m]
            low[i][k] = t * inv[k]
        t = cols[i][i]
        for m in range(i):
            t = t - low[i][m] * low[i][m]
        inv[i] = lax.rsqrt(t)
        u = pivots[i]
        for m in range(i):
            u = u - low[i][m] * made[m]
        made[i] = u * inv[i]
        put_r(at + i, made[i])
        if put_s:
            u = jnp.where(spot, jnp.where(lane == at + i, 1.0, 0.0).astype(f32), pivots[i])
            for m in range(i):
                u = u - low[i][m] * made_s[m]
            made_s[i] = u * inv[i]
            put_s(at + i, made_s[i])
    first = at + STEP
    if first == WIDTH:
        return
    back = [None] * STEP
    for i in reversed(range(STEP)):
        t = (made_s if put_s else made)[i]
        for m in range(i + 1, STEP):
            t = t - low[m][i] * back[m]
        back[i] = t * inv[i]

    def start(i):
        return jnp.where(spot, 0.0, get(i)) if put_s else get(i)

    later = first + STEP
    for i in range(first, later):
        row = get(i)
        put(i, start(i) - add_up([lane_copies(row, at + k) * back[k] for k in range(STEP)]))
    if later == WIDTH:
        return
    index = at + (lane % 64) // GROUP
    own = lane % GROUP == iota((GROUP, WIDTH), 0)
    left = []
    for i in range(later, WIDTH):
        value = jnp.take_along_axis(get(i), index, axis=1, mode="promise_in_bounds")
        value = jnp.where(own, value, 0.0)
        high = value.astype(bf16).astype(f32)
        left.append(jnp.where(lane < 64, high, value - high))
    left = jnp.concatenate(left, axis=0).astype(bf16)
    right = jnp.concatenate(split(jnp.concatenate(back, axis=0)), axis=1)
    right = jnp.concatenate([right, right], axis=0)
    out = lax.dot_general(left, right, (((1,), (0,)), ((), ())), preferred_element_type=f32)
    out = out[:, :WIDTH] + out[:, WIDTH:]
    for i in range(later, WIDTH):
        put(i, start(i) - out[GROUP * (i - later) : GROUP * (i - later + 1), :])


def position():
    return lax.axis_index("grp") * lax.axis_size("dev") + lax.axis_index("dev")


def local_kernel(
    counts_in, coords_in, proxies_in, leaf_in, node_in,
    basis_ref, gram_ref, heads_ref, message_ref, move_ref, columns_ref,
    counts, coords, proxies, leaf_t, node_t, sems,
):
    pairs = ((counts_in, counts), (coords_in, coords), (proxies_in, proxies), (leaf_in, leaf_t), (node_in, node_t))
    copies = [pltpu.make_async_copy(a, b, sems.at[i]) for i, (a, b) in enumerate(pairs)]
    for copy in copies:
        copy.start()
    leaves = basis_ref.shape[0]
    eye = unit(ridge)
    shape = (WIDTH, WIDTH)
    for copy in copies[:3]:
        copy.wait()
    grams = []
    lane = iota((1, WIDTH), 1)
    for leaf in range(leaves):
        span = slice(leaf * WIDTH, leaf * WIDTH + WIDTH)
        own = coords[:, span]
        valid = lane < counts[leaf]
        at = WIDTH + 3 * leaf
        message_ref[at : at + 1, :] = jnp.where(valid, own[0:1], -far)
        message_ref[at + 1 : at + 3, :] = own[1:3]
        turned = jnp.concatenate([jnp.where(valid, own[0:1], far), own[1:3], jnp.zeros((5, WIDTH), f32)], axis=0).T
        side = [jnp.broadcast_to(turned[:, d : d + 1], shape) for d in range(3)]
        for d in range(3):
            columns_ref[leaf, d] = side[d]
        basis = matern(*(side[d] - jnp.broadcast_to(proxies[d : d + 1, span], shape) for d in range(3)))
        basis_ref[leaf] = basis
        gram = product(basis, basis, 0, 0) * (1.0 / WIDTH) + eye
        gram_ref[pl.ds(leaf, WIDTH, stride=GROUP), :] = gram
        grams.append(gram)
    copies[3].wait()
    weights = [lift(leaf_t[leaf], grams[leaf]) for leaf in range(leaves)]
    copies[4].wait()
    move_ref[...] = node_t[0]
    heads_ref[pl.ds(GROUP - 1, WIDTH, stride=GROUP), :] = eye
    at = 0
    level = 1
    while len(weights) > 1:
        following = []
        for k in range(len(weights) // 2):
            head = weights[2 * k] + weights[2 * k + 1] + eye
            heads_ref[pl.ds(at, WIDTH, stride=GROUP), :] = head
            at += 1
            following.append(lift(node_t[k * 2**level + 2 ** (level - 1)], head))
        weights = following
        level += 1
    message_ref[0:WIDTH, :] = weights[0]


def lift_kernel(left, right, move, chosen_in, *rest, level):
    weight_ref, chosen_ref = rest[-2:]
    span = slice(0, WIDTH)
    head = left[span, :] + right[span, :] + unit(ridge)
    mine = position() % (2 ** (level + 1)) == 2**level
    chosen_ref[...] = jnp.where(mine, head, chosen_in[span, :])
    weight_ref[span, :] = lift(move[...], head)
    if weight_ref.shape[0] > WIDTH:
        weight_ref[WIDTH:, :] = right[WIDTH:, :]


def node_slots():
    slots = []
    level = 1
    while 2**level <= GROUP:
        slots += [k * 2**level + 2 ** (level - 1) for k in range(GROUP // 2**level)]
        level += 1
    return slots


class Copies:
    def __init__(self, sems):
        self.sems, self.made = sems, []

    def start(self, source, target):
        copy = pltpu.make_async_copy(source, target, self.sems.at[len(self.made)])
        copy.start()
        self.made.append(copy)

    def wait(self):
        for copy in self.made:
            copy.wait()


def near_part(near, flush, tiles_in, near_out, operands, tiles_out, wide, copies):
    for n, leaf in enumerate(flush):
        copies.start(tiles_in.at[n], near_out.at[leaf])
    if not near:
        return lambda t: None
    ids, message, low, high, columns = operands
    size = message.shape[0] - WIDTH
    leaves, fan = ids.shape[1], ids.shape[0]
    for n, ref in enumerate((low, message, high)):
        wide[n * size : (n + 1) * size, :] = ref[WIDTH:, :]
    offset = (position() - 1) * leaves
    shape = (WIDTH, WIDTH)

    def tile(t):
        if t >= len(near) * fan:
            return
        at, n = divmod(t, fan)
        leaf = near[at]
        other = wide[pl.ds(3 * (ids[n, leaf] - offset), 3), :]
        value = matern(*(columns[leaf, d] - jnp.broadcast_to(other[d : d + 1], shape) for d in range(3)))
        tiles_out[at, n] = value.astype(bf16)

    return tile


def work_kernel(*refs, names, steps, near, flush, final):
    ref = dict(zip(names, refs))
    copies = Copies(ref["sems"])
    tile = near_part(
        near, flush, ref.get("tiles_in"), ref.get("near_out"),
        [ref.get(n) for n in ("ids", "message", "low", "high", "columns")],
        ref.get("tiles_out"), ref.get("wide"), copies,
    )
    fan = ref["ids"].shape[0] if near else 0
    total = len(near) * fan
    share = -(-total // max(1, 2 * len(steps)))
    done = 0
    held = ({}, {})
    for s in steps:
        for side, name in enumerate(("leaf", "node")):
            source, values = ref[name + "_in"], held[side]
            base = STEP * steps[0]

            def get(i, source=source, values=values):
                return values[i] if i in values else rows_of(source, i)

            def put(i, value, values=values):
                values[i] = value

            def store(kind):
                target = ref[kind]

                def put_row(i, value):
                    target[GROUP * (i - base) : GROUP * (i - base + 1), :] = value

                return put_row

            eliminate(s, get, put, store(name + "_r"), store("leaf_s") if name == "leaf" else None)
            for t in range(done, done + share):
                tile(t)
            done += share
    for side, name in enumerate(("leaf", "node")):
        if name + "_out" in ref:
            for i in range(STEP * (steps[-1] + 1), WIDTH):
                ref[name + "_out"][GROUP * i : GROUP * (i + 1), :] = held[side][i]
    if final:
        parts = {
            kind: [ref[f"{kind}{n}"] for n in range(final)] for kind in ("leaf_r", "leaf_s", "node_r")
        }
        upper = iota((WIDTH, WIDTH), 1) >= iota((WIDTH, WIDTH), 0)
        lower = iota((WIDTH, WIDTH), 1) <= iota((WIDTH, WIDTH), 0)

        def whole(kind, b):
            return jnp.concatenate([stacked(part, b) for part in parts[kind]], axis=0)

        for b in range(GROUP):
            turned = jnp.where(lower, whole("leaf_s", b), 0.0)
            ref["bases"][b * WIDTH : (b + 1) * WIDTH, :] = product(ref["basis"][b], turned, 1, 1).astype(bf16)
            ref["factors"][b] = jnp.where(upper, whole("leaf_r", b), 0.0)
            copies.start(ref["factors"].at[b], ref["leaf_factors"].at[b])
            if b < GROUP - 1:
                ref["nodes"][b] = jnp.where(upper, whole("node_r", b), 0.0)
                copies.start(ref["nodes"].at[b], ref["node_factors"].at[node_slots()[b]])
        copies.start(ref["bases"], ref["leaf_bases"])
        for t in range(total):
            tile(t)
    copies.wait()


def top_kernel(*refs, names, flush, half):
    ref = dict(zip(names, refs))
    copies = Copies(ref["sems"])
    near_part((), flush, ref["tiles_in"], ref["near_out"], None, None, None, copies)
    left, right, chosen = ref["left"], ref["right"], ref["chosen"]
    top = jnp.where(position() % half == 0, left[...] + right[...] + unit(ridge), chosen[...])
    values = {}

    def get(i):
        return values[i] if i in values else jnp.broadcast_to(top[i : i + 1, :], (GROUP, WIDTH))

    def put(i, value):
        values[i] = value

    lane = iota((1, WIDTH), 1)
    target = ref["factor"]

    def put_r(i, value):
        target[i : i + 1, :] = jnp.where(lane >= i, value[0:1, :], 0.0)

    for s in range(STEPS):
        eliminate(s, get, put, put_r, None)
    copies.start(target, ref["node_out"].at[0])
    copies.wait()


def call(body, operands, outs, scratch, aliases, micros, name, **static):
    names = [o[0] for o in operands] + [o[0] for o in outs] + [s[0] for s in scratch]
    at = {o[0]: n for n, o in enumerate(operands)}
    to = {o[0]: n for n, o in enumerate(outs)}
    made = pl.pallas_call(
        functools.partial(body, names=names, **static),
        out_shape=[o[1] for o in outs],
        in_specs=[o[2] for o in operands],
        out_specs=[o[2] for o in outs],
        scratch_shapes=[s[1] for s in scratch],
        input_output_aliases={at[a]: to[b] for a, b in aliases.items()},
        compiler_params=params,
        cost_estimate=cost(micros),
        name=name,
    )(*(o[1] for o in operands))
    return dict(zip(to, made))


def shards(coords, counts, neighbours, proxies, leaf_transfers, node_transfers):
    leaves = counts.shape[0]
    slots = coords.shape[1] // leaves
    fan = neighbours.shape[0]
    count = lax.axis_size("grp") * lax.axis_size("dev")
    levels = count.bit_length() - 1
    half = count // 2
    both = ("grp", "dev")
    shape = jax.ShapeDtypeStruct
    mat = shape((WIDTH, WIDTH), f32)
    mats = shape((leaves, WIDTH, WIDTH), f32)
    flat = shape((WIDTH * GROUP, WIDTH), f32)
    long = shape((WIDTH + 3 * leaves, WIDTH), f32)

    basis, gram, heads, message, move, columns = pl.pallas_call(
        local_kernel,
        out_shape=(mats, flat, flat, long, mat, shape((leaves, 3, slots, WIDTH), f32)),
        in_specs=[anywhere] * 5,
        out_specs=(vmem,) * 6,
        scratch_shapes=[
            pltpu.SMEM(counts.shape, jnp.int32),
            pltpu.VMEM(coords.shape, f32),
            pltpu.VMEM(proxies.shape, f32),
            pltpu.VMEM(leaf_transfers.shape, f32),
            pltpu.VMEM(node_transfers.shape, f32),
            pltpu.SemaphoreType.DMA((5,)),
        ],
        compiler_params=params,
        cost_estimate=cost(4),
        name="local",
    )(*(pltpu.with_memory_space_constraint(x, pltpu.HBM) for x in (counts, coords, proxies, leaf_transfers, node_transfers)))

    plan = [
        dict(steps=(0, 1, 2, 3), near=()),
        dict(steps=(4, 5, 6, 7), near=()),
        dict(steps=(8, 9, 10, 11), near=(0, 1, 2)),
        dict(steps=(12, 13, 14, 15), near=(3, 4, 5)),
        dict(steps=(), near=tuple(range(6, leaves))),
    ]
    state = dict(leaf=gram, node=heads, parts=[], tiles=None, flush=(), near_out=None)

    def work(n, after, low, high):
        steps, near = plan[n]["steps"], plan[n]["near"]
        final = n == len(plan) - 1
        flush = state["flush"]
        operands = [("after", after, anywhere)]
        outs, scratch, aliases = [], [], {}
        if steps:
            rows = shape((STEP * len(steps) * GROUP, WIDTH), f32)
            operands += [("leaf_in", state["leaf"], vmem), ("node_in", state["node"], vmem)]
            outs += [(kind, rows, vmem) for kind in ("leaf_r", "leaf_s", "node_r")]
            if steps[-1] + 1 < STEPS:
                outs += [("leaf_out", flat, vmem), ("node_out", flat, vmem)]
        if near:
            operands += [("ids", neighbours, smem), ("message", message, vmem), ("low", low, vmem)]
            operands += [("high", high, vmem), ("columns", columns, vmem)]
            outs.append(("tiles_out", shape((len(near), fan, slots, slots), bf16), vmem))
            scratch.append(("wide", pltpu.VMEM((9 * leaves, WIDTH), f32)))
        if flush:
            operands.append(("tiles_in", state["tiles"], vmem))
            outs.append(("near_out", shape((leaves, fan, slots, slots), bf16), anywhere))
            if state["near_out"] is not None:
                operands.append(("near_in", state["near_out"], anywhere))
                aliases["near_in"] = "near_out"
        if final:
            for k, part in enumerate(state["parts"]):
                operands += [(f"{kind}{k}", part[kind], vmem) for kind in ("leaf_r", "leaf_s", "node_r")]
            operands.append(("basis", basis, vmem))
            outs += [("leaf_factors", mats, anywhere), ("node_factors", mats, anywhere)]
            outs.append(("leaf_bases", shape((leaves * slots, WIDTH), bf16), anywhere))
            scratch += [("factors", pltpu.VMEM(mats.shape, f32)), ("nodes", pltpu.VMEM(mats.shape, f32))]
            scratch.append(("bases", pltpu.VMEM((leaves * slots, WIDTH), bf16)))
        scratch.append(("sems", pltpu.SemaphoreType.DMA((32,))))
        made = call(
            work_kernel, operands, outs, scratch, aliases, 3, f"work{n}",
            steps=steps, near=near, flush=flush, final=len(state["parts"]) if final else 0,
        )
        if steps:
            state["parts"].append(made)
            state["leaf"], state["node"] = made.get("leaf_out"), made.get("node_out")
        state["tiles"], state["flush"] = made.get("tiles_out"), near
        state["near_out"] = made.get("near_out", state["near_out"])
        return made

    up = [(i, i + 1) for i in range(count - 1)]
    weight = chosen = message
    low = high = made = None
    for level in range(levels):
        span = 2 ** (level + 1)
        quarter = span // 4
        first = [(i + quarter, i + 2 * quarter) for i in range(0, count, span)]
        second = [(i + 3 * quarter, i + 2 * quarter) for i in range(0, count, span)]
        if level + 1 == levels:
            first.append((3 * quarter, 0))
            second.append((quarter, 0))
        if level == 0:
            left, right = lax.ppermute(weight, both, up), weight
            low = left
        elif level == 1:
            left = lax.ppermute(weight, both, first)
            right = lax.ppermute(weight, both, [(target, source) for source, target in up])
            high = right
        else:
            left, right = lax.ppermute(weight, both, first), lax.ppermute(weight, both, second)
        if level < len(plan):
            made = work(level, weight, low, high)
        if level + 1 < levels:
            outs = [("weight", long if level == 0 else mat, vmem), ("chosen_out", mat, vmem)]
            token = next(iter(made.values()))
            weight, chosen = pl.pallas_call(
                functools.partial(lift_kernel, level=level),
                out_shape=[o[1] for o in outs],
                in_specs=[vmem] * 4 + [anywhere],
                out_specs=[vmem] * 2,
                compiler_params=params,
                cost_estimate=cost(0.4),
                name=f"lift{level}",
            )(left, right, move, chosen, token)

    top = call(
        top_kernel,
        [
            ("left", left, vmem), ("right", right, vmem), ("chosen", chosen, vmem),
            ("tiles_in", state["tiles"], vmem), ("near_in", state["near_out"], anywhere),
            ("node_in", made["node_factors"], anywhere),
        ],
        [("near_out", shape((leaves, fan, slots, slots), bf16), anywhere), ("node_out", mats, anywhere)],
        [("factor", pltpu.VMEM((WIDTH, WIDTH), f32)), ("sems", pltpu.SemaphoreType.DMA((16,)))],
        {"near_in": "near_out", "node_in": "node_out"},
        5, "top", flush=state["flush"], half=half,
    )
    return (top["near_out"], made["leaf_bases"], made["leaf_factors"], top["node_out"])


def solution(mesh):
    both = ("grp", "dev")
    in_specs = (
        P(None, both),
        P(both),
        P(None, both),
        P(None, both),
        P(both, None, None),
        P(both, None, None),
    )
    out_specs = (
        P(both, None, None, None),
        P(both, None),
        P(both, None, None),
        P(both, None, None),
    )
    return jax.shard_map(shards, mesh=mesh, in_specs=in_specs, out_specs=out_specs, check_vma=False)
```

```python
import functools
import math

import jax
import jax.numpy as jnp
from jax import lax
from jax.experimental import pallas as pl
from jax.experimental.pallas import tpu as pltpu
from jax.sharding import PartitionSpec as P

ridge = 0.1
length_scale = 0.3
far = 1.0e6
f32 = jnp.float32
bf16 = jnp.bfloat16
STEP = 8
WIDTH = 128
GROUP = 8
STEPS = WIDTH // STEP
params = pltpu.CompilerParams(vmem_limit_bytes=40 * 1024 * 1024)
vmem = pl.BlockSpec(memory_space=pltpu.VMEM)
smem = pl.BlockSpec(memory_space=pltpu.SMEM)
anywhere = pl.BlockSpec(memory_space=pl.ANY)


def cost(micros):
    return pl.CostEstimate(flops=int(micros * 1.0e9), bytes_accessed=int(micros * 3.0e6), transcendentals=0)


def iota(shape, dim):
    return lax.broadcasted_iota(jnp.int32, shape, dim)


def split(value):
    high = value.astype(bf16)
    return high, (value - high.astype(f32)).astype(bf16)


def product(left, right, left_dim, right_dim):
    def dot(a, b):
        return lax.dot_general(a, b, (((left_dim,), (right_dim,)), ((), ())), preferred_element_type=f32)

    (lh, ll), (rh, rl) = split(left), split(right)
    return dot(lh, rh) + (dot(lh, rl) + dot(ll, rh))


def lift(move, head):
    return product(move, product(head, move, 1, 0), 0, 0)


def unit(scale):
    shape = (WIDTH, WIDTH)
    return jnp.where(iota(shape, 0) == iota(shape, 1), scale, 0.0).astype(f32)


def matern(delta_x, delta_y, delta_z):
    scale = 3.0**0.5 / length_scale * math.log2(math.e)
    square = delta_x * delta_x + delta_y * delta_y + delta_z * delta_z
    square = jnp.maximum(square * (scale * scale), 1e-30)
    u = square * lax.rsqrt(square)
    return (1.0 + u * math.log(2.0)) * jnp.exp2(-u)


def lane_copies(vreg, lane):
    return jnp.broadcast_to(vreg[:, lane : lane + 1], vreg.shape)


def add_up(terms):
    while len(terms) > 1:
        terms = [
            terms[a] + terms[a + 1] if a + 1 < len(terms) else terms[a] for a in range(0, len(terms), 2)
        ]
    return terms[0]


def rows_of(ref, i):
    return ref[GROUP * i : GROUP * (i + 1), :]


def stacked(ref, matrix):
    return ref[pl.ds(matrix, ref.shape[0] // GROUP, stride=GROUP), :]


def eliminate(s, get, put, put_r, put_s):
    at = STEP * s
    lane = iota((GROUP, WIDTH), 1)
    pivots = [get(at + i) for i in range(STEP)]
    cols = [[lane_copies(pivots[i], at + k) for k in range(i + 1)] for i in range(STEP)]
    spot = (lane >= at) & (lane < at + STEP)
    low = [[None] * STEP for _ in range(STEP)]
    inv = [None] * STEP
    made = [None] * STEP
    made_s = [None] * STEP
    for i in range(STEP):
        for k in range(i):
            t = cols[i][k]
            for m in range(k):
                t = t - low[i][m] * low[k][m]
            low[i][k] = t * inv[k]
        t = cols[i][i]
        for m in range(i):
            t = t - low[i][m] * low[i][m]
        inv[i] = lax.rsqrt(t)
        u = pivots[i]
        for m in range(i):
            u = u - low[i][m] * made[m]
        made[i] = u * inv[i]
        put_r(at + i, made[i])
        if put_s:
            u = jnp.where(spot, jnp.where(lane == at + i, 1.0, 0.0).astype(f32), pivots[i])
            for m in range(i):
                u = u - low[i][m] * made_s[m]
            made_s[i] = u * inv[i]
            put_s(at + i, made_s[i])
    first = at + STEP
    if first == WIDTH:
        return
    back = [None] * STEP
    for i in reversed(range(STEP)):
        t = (made_s if put_s else made)[i]
        for m in range(i + 1, STEP):
            t = t - low[m][i] * back[m]
        back[i] = t * inv[i]

    def start(i):
        return jnp.where(spot, 0.0, get(i)) if put_s else get(i)

    later = first + STEP
    for i in range(first, later):
        row = get(i)
        put(i, start(i) - add_up([lane_copies(row, at + k) * back[k] for k in range(STEP)]))
    if later == WIDTH:
        return
    index = at + (lane % 64) // GROUP
    own = lane % GROUP == iota((GROUP, WIDTH), 0)
    left = []
    for i in range(later, WIDTH):
        value = jnp.take_along_axis(get(i), index, axis=1, mode="promise_in_bounds")
        value = jnp.where(own, value, 0.0)
        high = value.astype(bf16).astype(f32)
        left.append(jnp.where(lane < 64, high, value - high))
    left = jnp.concatenate(left, axis=0).astype(bf16)
    right = jnp.concatenate(split(jnp.concatenate(back, axis=0)), axis=1)
    right = jnp.concatenate([right, right], axis=0)
    out = lax.dot_general(left, right, (((1,), (0,)), ((), ())), preferred_element_type=f32)
    out = out[:, :WIDTH] + out[:, WIDTH:]
    for i in range(later, WIDTH):
        put(i, start(i) - out[GROUP * (i - later) : GROUP * (i - later + 1), :])


def position():
    return lax.axis_index("grp") * lax.axis_size("dev") + lax.axis_index("dev")


def local_kernel(
    counts_in, coords_in, proxies_in, leaf_in, node_in,
    basis_ref, gram_ref, heads_ref, weight_ref, message_ref, move_ref, columns_ref,
    counts, coords, proxies, leaf_t, node_t, sems,
):
    pairs = ((counts_in, counts), (coords_in, coords), (proxies_in, proxies), (leaf_in, leaf_t), (node_in, node_t))
    copies = [pltpu.make_async_copy(a, b, sems.at[i]) for i, (a, b) in enumerate(pairs)]
    for copy in copies:
        copy.start()
    leaves = basis_ref.shape[0]
    eye = unit(ridge)
    shape = (WIDTH, WIDTH)
    for copy in copies[:3]:
        copy.wait()
    grams = []
    lane = iota((1, WIDTH), 1)
    for leaf in range(leaves):
        span = slice(leaf * WIDTH, leaf * WIDTH + WIDTH)
        own = coords[:, span]
        valid = lane < counts[leaf]
        at = 3 * leaf
        message_ref[at : at + 1, :] = jnp.where(valid, own[0:1], -far)
        message_ref[at + 1 : at + 3, :] = own[1:3]
        turned = jnp.concatenate([jnp.where(valid, own[0:1], far), own[1:3], jnp.zeros((5, WIDTH), f32)], axis=0).T
        side = [jnp.broadcast_to(turned[:, d : d + 1], shape) for d in range(3)]
        for d in range(3):
            columns_ref[leaf, d] = side[d]
        basis = matern(*(side[d] - jnp.broadcast_to(proxies[d : d + 1, span], shape) for d in range(3)))
        basis_ref[leaf] = basis
        gram = product(basis, basis, 0, 0) * (1.0 / WIDTH) + eye
        gram_ref[pl.ds(leaf, WIDTH, stride=GROUP), :] = gram
        grams.append(gram)
    copies[3].wait()
    weights = [lift(leaf_t[leaf], grams[leaf]) for leaf in range(leaves)]
    copies[4].wait()
    move_ref[...] = node_t[0]
    heads_ref[pl.ds(GROUP - 1, WIDTH, stride=GROUP), :] = eye
    at = 0
    level = 1
    while len(weights) > 1:
        following = []
        for k in range(len(weights) // 2):
            head = weights[2 * k] + weights[2 * k + 1] + eye
            heads_ref[pl.ds(at, WIDTH, stride=GROUP), :] = head
            at += 1
            following.append(lift(node_t[k * 2**level + 2 ** (level - 1)], head))
        weights = following
        level += 1
    weight_ref[...] = weights[0]


def lift_kernel(left, right, move, chosen_in, token, weight_ref, chosen_ref, *, level):
    del token
    head = left[...] + right[...] + unit(ridge)
    mine = position() % (2 ** (level + 1)) == 2**level
    chosen_ref[...] = jnp.where(mine, head, chosen_in[...])
    weight_ref[...] = lift(move[...], head)


def node_slots():
    slots = []
    level = 1
    while 2**level <= GROUP:
        slots += [k * 2**level + 2 ** (level - 1) for k in range(GROUP // 2**level)]
        level += 1
    return slots


class Copies:
    def __init__(self, sems):
        self.sems, self.made = sems, []

    def start(self, source, target):
        copy = pltpu.make_async_copy(source, target, self.sems.at[len(self.made)])
        copy.start()
        self.made.append(copy)

    def wait(self):
        for copy in self.made:
            copy.wait()


def work_kernel(*refs, names, steps, final):
    ref = dict(zip(names, refs))
    held = ({}, {})
    for s in steps:
        for side, name in enumerate(("leaf", "node")):
            source, values = ref[name + "_in"], held[side]
            base = STEP * steps[0]

            def get(i, source=source, values=values):
                return values[i] if i in values else rows_of(source, i)

            def put(i, value, values=values):
                values[i] = value

            def store(kind):
                target = ref[kind]

                def put_row(i, value):
                    target[GROUP * (i - base) : GROUP * (i - base + 1), :] = value

                return put_row

            eliminate(s, get, put, store(name + "_r"), store("leaf_s") if name == "leaf" else None)
    for side, name in enumerate(("leaf", "node")):
        if name + "_out" in ref:
            for i in range(STEP * (steps[-1] + 1), WIDTH):
                ref[name + "_out"][GROUP * i : GROUP * (i + 1), :] = held[side][i]
    if "own" in ref:
        ref["own"][...] = ref["message"][...]
    if not final:
        return
    copies = Copies(ref["sems"])
    parts = {kind: [ref[f"{kind}{n}"] for n in range(final)] for kind in ("leaf_r", "leaf_s", "node_r")}
    upper = iota((WIDTH, WIDTH), 1) >= iota((WIDTH, WIDTH), 0)
    lower = iota((WIDTH, WIDTH), 1) <= iota((WIDTH, WIDTH), 0)

    def whole(kind, b):
        return jnp.concatenate([stacked(part, b) for part in parts[kind]], axis=0)

    for b in range(GROUP):
        ref["factors"][b] = jnp.where(upper, whole("leaf_r", b), 0.0)
        copies.start(ref["factors"].at[b], ref["leaf_factors"].at[b])
        if b < GROUP - 1:
            ref["nodes"][b] = jnp.where(upper, whole("node_r", b), 0.0)
            copies.start(ref["nodes"].at[b], ref["node_factors"].at[node_slots()[b]])
    for b in range(GROUP):
        span = pl.ds(b * WIDTH, WIDTH)
        turned = jnp.where(lower, whole("leaf_s", b), 0.0)
        ref["bases"][span, :] = product(ref["basis"][b], turned, 1, 1).astype(bf16)
        copies.start(ref["bases"].at[span, :], ref["leaf_bases"].at[span, :])
    copies.wait()


def top_kernel(*refs, names, half):
    ref = dict(zip(names, refs))
    copies = Copies(ref["sems"])
    ids, columns, tiles, wide = ref["ids"], ref["columns"], ref["tiles"], ref["wide"]
    leaves, fan = ids.shape[1], ids.shape[0]
    size = ref["own"].shape[0]
    for n, name in enumerate(("low", "own", "high")):
        wide[n * size : (n + 1) * size, :] = ref[name][...]
    offset = (position() - 1) * leaves

    def tile(t):
        leaf, n = divmod(t, fan)
        other = wide[pl.ds(3 * (ids[n, leaf] - offset), 3), :]
        shape = (WIDTH, WIDTH)
        value = matern(*(columns[leaf, d] - jnp.broadcast_to(other[d : d + 1], shape) for d in range(3)))
        tiles[leaf, n] = value.astype(bf16)
        if n == fan - 1:
            copies.start(tiles.at[leaf], ref["near_out"].at[leaf])

    left, right, chosen = ref["left"], ref["right"], ref["chosen"]
    top = jnp.where(position() % half == 0, left[...] + right[...] + unit(ridge), chosen[...])
    values = {}

    def get(i):
        return values[i] if i in values else jnp.broadcast_to(top[i : i + 1, :], (GROUP, WIDTH))

    def put(i, value):
        values[i] = value

    lane = iota((1, WIDTH), 1)
    target = ref["factor"]

    def put_r(i, value):
        target[i : i + 1, :] = jnp.where(lane >= i, value[0:1, :], 0.0)

    total = leaves * fan
    share = -(-total // (STEPS - 2))
    for s in range(STEPS):
        eliminate(s, get, put, put_r, None)
        for t in range(s * share, min((s + 1) * share, total)):
            tile(t)
    copies.start(target, ref["node_out"].at[0])
    copies.wait()


def call(body, operands, outs, scratch, aliases, micros, name, **static):
    names = [o[0] for o in operands] + [o[0] for o in outs] + [s[0] for s in scratch]
    at = {o[0]: n for n, o in enumerate(operands)}
    to = {o[0]: n for n, o in enumerate(outs)}
    made = pl.pallas_call(
        functools.partial(body, names=names, **static),
        out_shape=[o[1] for o in outs],
        in_specs=[o[2] for o in operands],
        out_specs=[o[2] for o in outs],
        scratch_shapes=[s[1] for s in scratch],
        input_output_aliases={at[a]: to[b] for a, b in aliases.items()},
        compiler_params=params,
        cost_estimate=cost(micros),
        name=name,
    )(*(o[1] for o in operands))
    return dict(zip(to, made))


def shards(coords, counts, neighbours, proxies, leaf_transfers, node_transfers):
    leaves = counts.shape[0]
    slots = coords.shape[1] // leaves
    fan = neighbours.shape[0]
    count = lax.axis_size("grp") * lax.axis_size("dev")
    levels = count.bit_length() - 1
    half = count // 2
    both = ("grp", "dev")
    shape = jax.ShapeDtypeStruct
    mat = shape((WIDTH, WIDTH), f32)
    mats = shape((leaves, WIDTH, WIDTH), f32)
    flat = shape((WIDTH * GROUP, WIDTH), f32)
    coords_shape = shape((3 * leaves, WIDTH), f32)
    halo_level = 3

    basis, gram, heads, weight_own, message, move, columns = pl.pallas_call(
        local_kernel,
        out_shape=(mats, flat, flat, mat, coords_shape, mat, shape((leaves, 3, slots, WIDTH), f32)),
        in_specs=[anywhere] * 5,
        out_specs=(vmem,) * 7,
        scratch_shapes=[
            pltpu.SMEM(counts.shape, jnp.int32),
            pltpu.VMEM(coords.shape, f32),
            pltpu.VMEM(proxies.shape, f32),
            pltpu.VMEM(leaf_transfers.shape, f32),
            pltpu.VMEM(node_transfers.shape, f32),
            pltpu.SemaphoreType.DMA((5,)),
        ],
        compiler_params=params,
        cost_estimate=cost(4),
        name="local",
    )(*(pltpu.with_memory_space_constraint(x, pltpu.HBM) for x in (counts, coords, proxies, leaf_transfers, node_transfers)))

    plan = [(0, 1, 2, 3), (4, 5, 6, 7), (8, 9, 10, 11), (12, 13, 14, 15), ()]
    state = dict(leaf=gram, node=heads)
    parts = []

    def work(n, after):
        steps = plan[n]
        final = n == len(plan) - 1
        operands = [("after", after, anywhere)]
        outs, scratch = [], []
        if steps:
            rows = shape((STEP * len(steps) * GROUP, WIDTH), f32)
            operands += [("leaf_in", state["leaf"], vmem), ("node_in", state["node"], vmem)]
            outs += [(kind, rows, vmem) for kind in ("leaf_r", "leaf_s", "node_r")]
            if steps[-1] + 1 < STEPS:
                outs += [("leaf_out", flat, vmem), ("node_out", flat, vmem)]
        if n == halo_level:
            operands.append(("message", message, vmem))
            outs.append(("own", coords_shape, vmem))
        if final:
            for k, part in enumerate(parts):
                operands += [(f"{kind}{k}", part[kind], vmem) for kind in ("leaf_r", "leaf_s", "node_r")]
            operands.append(("basis", basis, vmem))
            outs += [("leaf_factors", mats, anywhere), ("node_factors", mats, anywhere)]
            outs.append(("leaf_bases", shape((leaves * slots, WIDTH), bf16), anywhere))
            scratch += [("factors", pltpu.VMEM(mats.shape, f32)), ("nodes", pltpu.VMEM(mats.shape, f32))]
            scratch.append(("bases", pltpu.VMEM((leaves * slots, WIDTH), bf16)))
            scratch.append(("sems", pltpu.SemaphoreType.DMA((3 * GROUP,))))
        made = call(
            work_kernel, operands, outs, scratch, {}, 3, f"work{n}",
            steps=steps, final=len(parts) if final else 0,
        )
        if steps:
            parts.append(made)
            state["leaf"], state["node"] = made.get("leaf_out"), made.get("node_out")
        return made

    weight = chosen = weight_own
    made = low = high = own = None
    for level in range(levels):
        span = 2 ** (level + 1)
        quarter = span // 4
        if level == 0:
            left, right = lax.ppermute(weight, both, [(i, i + 1) for i in range(0, count, 2)]), weight
        else:
            first = [(i + quarter, i + 2 * quarter) for i in range(0, count, span)]
            second = [(i + 3 * quarter, i + 2 * quarter) for i in range(0, count, span)]
            if level + 1 == levels:
                first.append((3 * quarter, 0))
                second.append((quarter, 0))
            left, right = lax.ppermute(weight, both, first), lax.ppermute(weight, both, second)
        if level < len(plan):
            made = work(level, weight)
        if level == halo_level:
            own = made["own"]
            up = [(i, i + 1) for i in range(count - 1)]
            low = lax.ppermute(own, both, up)
            high = lax.ppermute(own, both, [(target, source) for source, target in up])
        if level + 1 < levels:
            weight, chosen = pl.pallas_call(
                functools.partial(lift_kernel, level=level),
                out_shape=[mat, mat],
                in_specs=[vmem] * 4 + [anywhere],
                out_specs=[vmem] * 2,
                compiler_params=params,
                cost_estimate=cost(0.4),
                name=f"lift{level}",
            )(left, right, move, chosen, next(iter(made.values())))

    top = call(
        top_kernel,
        [
            ("left", left, vmem), ("right", right, vmem), ("chosen", chosen, vmem), ("ids", neighbours, smem),
            ("own", own, vmem), ("low", low, vmem), ("high", high, vmem), ("columns", columns, vmem),
            ("node_in", made["node_factors"], anywhere),
        ],
        [("near_out", shape((leaves, fan, slots, slots), bf16), anywhere), ("node_out", mats, anywhere)],
        [
            ("factor", pltpu.VMEM((WIDTH, WIDTH), f32)),
            ("tiles", pltpu.VMEM((leaves, fan, slots, slots), bf16)),
            ("wide", pltpu.VMEM((9 * leaves, WIDTH), f32)),
            ("sems", pltpu.SemaphoreType.DMA((leaves + 1,))),
        ],
        {"node_in": "node_out"},
        6, "top", half=half,
    )
    return (top["near_out"], made["leaf_bases"], made["leaf_factors"], top["node_out"])


def solution(mesh):
    both = ("grp", "dev")
    in_specs = (
        P(None, both),
        P(both),
        P(None, both),
        P(None, both),
        P(both, None, None),
        P(both, None, None),
    )
    out_specs = (
        P(both, None, None, None),
        P(both, None),
        P(both, None, None),
        P(both, None, None),
    )
    return jax.shard_map(shards, mesh=mesh, in_specs=in_specs, out_specs=out_specs, check_vma=False)
```

```python
import functools
import math

import jax
import jax.numpy as jnp
from jax import lax
from jax.experimental import pallas as pl
from jax.experimental.pallas import tpu as pltpu
from jax.sharding import PartitionSpec as P

ridge = 0.1
length_scale = 0.3
far = 1.0e6
f32 = jnp.float32
bf16 = jnp.bfloat16
STEP = 8
WIDTH = 128
GROUP = 8
STEPS = WIDTH // STEP
params = pltpu.CompilerParams(vmem_limit_bytes=40 * 1024 * 1024)
vmem = pl.BlockSpec(memory_space=pltpu.VMEM)
smem = pl.BlockSpec(memory_space=pltpu.SMEM)
anywhere = pl.BlockSpec(memory_space=pl.ANY)


def cost(micros):
    return pl.CostEstimate(flops=int(micros * 1.0e9), bytes_accessed=int(micros * 3.0e6), transcendentals=0)


def iota(shape, dim):
    return lax.broadcasted_iota(jnp.int32, shape, dim)


def split(value):
    high = value.astype(bf16)
    return high, (value - high.astype(f32)).astype(bf16)


def product(left, right, left_dim, right_dim):
    def dot(a, b):
        return lax.dot_general(a, b, (((left_dim,), (right_dim,)), ((), ())), preferred_element_type=f32)

    (lh, ll), (rh, rl) = split(left), split(right)
    return dot(lh, rh) + (dot(lh, rl) + dot(ll, rh))


def lift(move, head):
    return product(move, product(head, move, 1, 0), 0, 0)


def unit(scale):
    shape = (WIDTH, WIDTH)
    return jnp.where(iota(shape, 0) == iota(shape, 1), scale, 0.0).astype(f32)


def matern(delta_x, delta_y, delta_z):
    scale = 3.0**0.5 / length_scale * math.log2(math.e)
    square = delta_x * delta_x + delta_y * delta_y + delta_z * delta_z
    square = jnp.maximum(square * (scale * scale), 1e-30)
    u = square * lax.rsqrt(square)
    return (1.0 + u * math.log(2.0)) * jnp.exp2(-u)


def lane_copies(vreg, lane):
    return jnp.broadcast_to(vreg[:, lane : lane + 1], vreg.shape)


def add_up(terms):
    while len(terms) > 1:
        terms = [
            terms[a] + terms[a + 1] if a + 1 < len(terms) else terms[a] for a in range(0, len(terms), 2)
        ]
    return terms[0]


def rows_of(ref, i):
    return ref[GROUP * i : GROUP * (i + 1), :]


def stacked(ref, matrix):
    return ref[pl.ds(matrix, ref.shape[0] // GROUP, stride=GROUP), :]


def eliminate(s, get, put, put_r, put_s):
    at = STEP * s
    lane = iota((GROUP, WIDTH), 1)
    pivots = [get(at + i) for i in range(STEP)]
    cols = [[lane_copies(pivots[i], at + k) for k in range(i + 1)] for i in range(STEP)]
    spot = (lane >= at) & (lane < at + STEP)
    low = [[None] * STEP for _ in range(STEP)]
    inv = [None] * STEP
    made = [None] * STEP
    made_s = [None] * STEP
    for i in range(STEP):
        for k in range(i):
            t = cols[i][k]
            for m in range(k):
                t = t - low[i][m] * low[k][m]
            low[i][k] = t * inv[k]
        t = cols[i][i]
        for m in range(i):
            t = t - low[i][m] * low[i][m]
        inv[i] = lax.rsqrt(t)
        u = pivots[i]
        for m in range(i):
            u = u - low[i][m] * made[m]
        made[i] = u * inv[i]
        put_r(at + i, made[i])
        if put_s:
            u = jnp.where(spot, jnp.where(lane == at + i, 1.0, 0.0).astype(f32), pivots[i])
            for m in range(i):
                u = u - low[i][m] * made_s[m]
            made_s[i] = u * inv[i]
            put_s(at + i, made_s[i])
    first = at + STEP
    if first == WIDTH:
        return
    back = [None] * STEP
    for i in reversed(range(STEP)):
        t = (made_s if put_s else made)[i]
        for m in range(i + 1, STEP):
            t = t - low[m][i] * back[m]
        back[i] = t * inv[i]

    def start(i):
        return jnp.where(spot, 0.0, get(i)) if put_s else get(i)

    later = first + STEP
    for i in range(first, later):
        row = get(i)
        put(i, start(i) - add_up([lane_copies(row, at + k) * back[k] for k in range(STEP)]))
    if later == WIDTH:
        return
    index = at + (lane % 64) // GROUP
    own = lane % GROUP == iota((GROUP, WIDTH), 0)
    left = []
    for i in range(later, WIDTH):
        value = jnp.take_along_axis(get(i), index, axis=1, mode="promise_in_bounds")
        value = jnp.where(own, value, 0.0)
        high = value.astype(bf16).astype(f32)
        left.append(jnp.where(lane < 64, high, value - high))
    left = jnp.concatenate(left, axis=0).astype(bf16)
    right = jnp.concatenate(split(jnp.concatenate(back, axis=0)), axis=1)
    right = jnp.concatenate([right, right], axis=0)
    out = lax.dot_general(left, right, (((1,), (0,)), ((), ())), preferred_element_type=f32)
    out = out[:, :WIDTH] + out[:, WIDTH:]
    for i in range(later, WIDTH):
        put(i, start(i) - out[GROUP * (i - later) : GROUP * (i - later + 1), :])


def position():
    return lax.axis_index("grp") * lax.axis_size("dev") + lax.axis_index("dev")


def local_kernel(
    counts_in, coords_in, proxies_in, leaf_in, node_in,
    basis_ref, gram_ref, heads_ref, weight_ref, message_ref, move_ref, columns_ref,
    counts, coords, proxies, leaf_t, node_t, sems,
):
    pairs = ((counts_in, counts), (coords_in, coords), (proxies_in, proxies), (leaf_in, leaf_t), (node_in, node_t))
    copies = [pltpu.make_async_copy(a, b, sems.at[i]) for i, (a, b) in enumerate(pairs)]
    for copy in copies:
        copy.start()
    leaves = basis_ref.shape[0]
    eye = unit(ridge)
    shape = (WIDTH, WIDTH)
    for copy in copies[:3]:
        copy.wait()
    grams = []
    lane = iota((1, WIDTH), 1)
    for leaf in range(leaves):
        span = slice(leaf * WIDTH, leaf * WIDTH + WIDTH)
        own = coords[:, span]
        valid = lane < counts[leaf]
        at = 3 * leaf
        message_ref[at : at + 1, :] = jnp.where(valid, own[0:1], -far)
        message_ref[at + 1 : at + 3, :] = own[1:3]
        turned = jnp.concatenate([jnp.where(valid, own[0:1], far), own[1:3], jnp.zeros((5, WIDTH), f32)], axis=0).T
        side = [jnp.broadcast_to(turned[:, d : d + 1], shape) for d in range(3)]
        for d in range(3):
            columns_ref[leaf, d] = side[d]
        basis = matern(*(side[d] - jnp.broadcast_to(proxies[d : d + 1, span], shape) for d in range(3)))
        basis_ref[leaf] = basis
        gram = product(basis, basis, 0, 0) * (1.0 / WIDTH) + eye
        gram_ref[pl.ds(leaf, WIDTH, stride=GROUP), :] = gram
        grams.append(gram)
    copies[3].wait()
    weights = [lift(leaf_t[leaf], grams[leaf]) for leaf in range(leaves)]
    copies[4].wait()
    move_ref[...] = node_t[0]
    heads_ref[pl.ds(GROUP - 1, WIDTH, stride=GROUP), :] = eye
    at = 0
    level = 1
    while len(weights) > 1:
        following = []
        for k in range(len(weights) // 2):
            head = weights[2 * k] + weights[2 * k + 1] + eye
            heads_ref[pl.ds(at, WIDTH, stride=GROUP), :] = head
            at += 1
            following.append(lift(node_t[k * 2**level + 2 ** (level - 1)], head))
        weights = following
        level += 1
    weight_ref[...] = weights[0]


def lift_kernel(left, right, move, chosen_in, token, weight_ref, chosen_ref, *, level):
    del token
    head = left[...] + right[...] + unit(ridge)
    mine = position() % (2 ** (level + 1)) == 2**level
    chosen_ref[...] = jnp.where(mine, head, chosen_in[...])
    weight_ref[...] = lift(move[...], head)


def node_slots():
    slots = []
    level = 1
    while 2**level <= GROUP:
        slots += [k * 2**level + 2 ** (level - 1) for k in range(GROUP // 2**level)]
        level += 1
    return slots


class Copies:
    def __init__(self, sems):
        self.sems, self.made = sems, []

    def start(self, source, target):
        copy = pltpu.make_async_copy(source, target, self.sems.at[len(self.made)])
        copy.start()
        self.made.append(copy)

    def wait(self):
        for copy in self.made:
            copy.wait()


def near_tiles(ref, near, copies):
    ids, columns, tiles, wide = ref["ids"], ref["columns"], ref["tiles"], ref["wide"]
    leaves, fan = ids.shape[1], ids.shape[0]
    size = ref["own"].shape[0]
    for n, name in enumerate(("low", "own", "high")):
        wide[n * size : (n + 1) * size, :] = ref[name][...]
    offset = (position() - 1) * leaves
    total = len(near) * fan

    def tile(t):
        at, n = divmod(t, fan)
        leaf = near[at]
        other = wide[pl.ds(3 * (ids[n, leaf] - offset), 3), :]
        shape = (WIDTH, WIDTH)
        value = matern(*(columns[leaf, d] - jnp.broadcast_to(other[d : d + 1], shape) for d in range(3)))
        tiles[at, n] = value.astype(bf16)
        if n == fan - 1:
            copies.start(tiles.at[at], ref["near_out"].at[leaf])

    return tile, total


def work_kernel(*refs, names, steps, near, final):
    ref = dict(zip(names, refs))
    held = ({}, {})
    copies = Copies(ref["sems"]) if "sems" in ref else None
    tile, total = near_tiles(ref, near, copies) if near else (None, 0)
    done = 0
    share = -(-total // max(1, len(steps) - 1)) if steps else total
    for s in steps:
        for side, name in enumerate(("leaf", "node")):
            source, values = ref[name + "_in"], held[side]
            base = STEP * steps[0]

            def get(i, source=source, values=values):
                return values[i] if i in values else rows_of(source, i)

            def put(i, value, values=values):
                values[i] = value

            def store(kind):
                target = ref[kind]

                def put_row(i, value):
                    target[GROUP * (i - base) : GROUP * (i - base + 1), :] = value

                return put_row

            eliminate(s, get, put, store(name + "_r"), store("leaf_s") if name == "leaf" else None)
            if side == 0:
                for t in range(done, min(done + share, total)):
                    tile(t)
                done += share
    for side, name in enumerate(("leaf", "node")):
        if name + "_out" in ref:
            for i in range(STEP * (steps[-1] + 1), WIDTH):
                ref[name + "_out"][GROUP * i : GROUP * (i + 1), :] = held[side][i]
    if "message" in ref:
        ref["own"][...] = ref["message"][...]
    if not final:
        if copies:
            copies.wait()
        return
    if not steps:
        for t in range(total):
            tile(t)
    parts = {kind: [ref[f"{kind}{n}"] for n in range(final)] for kind in ("leaf_r", "leaf_s", "node_r")}
    upper = iota((WIDTH, WIDTH), 1) >= iota((WIDTH, WIDTH), 0)
    lower = iota((WIDTH, WIDTH), 1) <= iota((WIDTH, WIDTH), 0)

    def whole(kind, b):
        return jnp.concatenate([stacked(part, b) for part in parts[kind]], axis=0)

    for b in range(GROUP):
        ref["factors"][b] = jnp.where(upper, whole("leaf_r", b), 0.0)
        copies.start(ref["factors"].at[b], ref["leaf_factors"].at[b])
        if b < GROUP - 1:
            ref["nodes"][b] = jnp.where(upper, whole("node_r", b), 0.0)
            copies.start(ref["nodes"].at[b], ref["node_factors"].at[node_slots()[b]])
    for b in range(GROUP):
        span = pl.ds(b * WIDTH, WIDTH)
        turned = jnp.where(lower, whole("leaf_s", b), 0.0)
        ref["bases"][span, :] = product(ref["basis"][b], turned, 1, 1).astype(bf16)
        copies.start(ref["bases"].at[span, :], ref["leaf_bases"].at[span, :])
    copies.wait()


def top_kernel(*refs, names, near, half):
    ref = dict(zip(names, refs))
    copies = Copies(ref["sems"])
    tile, total = near_tiles(ref, near, copies)
    left, right, chosen = ref["left"], ref["right"], ref["chosen"]
    top = jnp.where(position() % half == 0, left[...] + right[...] + unit(ridge), chosen[...])
    values = {}

    def get(i):
        return values[i] if i in values else jnp.broadcast_to(top[i : i + 1, :], (GROUP, WIDTH))

    def put(i, value):
        values[i] = value

    lane = iota((1, WIDTH), 1)
    target = ref["factor"]

    def put_r(i, value):
        target[i : i + 1, :] = jnp.where(lane >= i, value[0:1, :], 0.0)

    share = -(-total // (STEPS - 4))
    for s in range(STEPS):
        eliminate(s, get, put, put_r, None)
        for t in range(s * share, min((s + 1) * share, total)):
            tile(t)
    copies.start(target, ref["node_out"].at[0])
    copies.wait()


def call(body, operands, outs, scratch, aliases, micros, name, **static):
    names = [o[0] for o in operands] + [o[0] for o in outs] + [s[0] for s in scratch]
    at = {o[0]: n for n, o in enumerate(operands)}
    to = {o[0]: n for n, o in enumerate(outs)}
    made = pl.pallas_call(
        functools.partial(body, names=names, **static),
        out_shape=[o[1] for o in outs],
        in_specs=[o[2] for o in operands],
        out_specs=[o[2] for o in outs],
        scratch_shapes=[s[1] for s in scratch],
        input_output_aliases={at[a]: to[b] for a, b in aliases.items()},
        compiler_params=params,
        cost_estimate=cost(micros),
        name=name,
    )(*(o[1] for o in operands))
    return dict(zip(to, made))


def shards(coords, counts, neighbours, proxies, leaf_transfers, node_transfers):
    leaves = counts.shape[0]
    slots = coords.shape[1] // leaves
    fan = neighbours.shape[0]
    count = lax.axis_size("grp") * lax.axis_size("dev")
    levels = count.bit_length() - 1
    half = count // 2
    both = ("grp", "dev")
    shape = jax.ShapeDtypeStruct
    mat = shape((WIDTH, WIDTH), f32)
    mats = shape((leaves, WIDTH, WIDTH), f32)
    flat = shape((WIDTH * GROUP, WIDTH), f32)
    coords_shape = shape((3 * leaves, WIDTH), f32)

    basis, gram, heads, weight_own, message, move, columns = pl.pallas_call(
        local_kernel,
        out_shape=(mats, flat, flat, mat, coords_shape, mat, shape((leaves, 3, slots, WIDTH), f32)),
        in_specs=[anywhere] * 5,
        out_specs=(vmem,) * 7,
        scratch_shapes=[
            pltpu.SMEM(counts.shape, jnp.int32),
            pltpu.VMEM(coords.shape, f32),
            pltpu.VMEM(proxies.shape, f32),
            pltpu.VMEM(leaf_transfers.shape, f32),
            pltpu.VMEM(node_transfers.shape, f32),
            pltpu.SemaphoreType.DMA((5,)),
        ],
        compiler_params=params,
        cost_estimate=cost(4),
        name="local",
    )(*(pltpu.with_memory_space_constraint(x, pltpu.HBM) for x in (counts, coords, proxies, leaf_transfers, node_transfers)))

    plan = [
        ((0, 1, 2, 3), ()),
        ((4, 5, 6, 7), ()),
        ((8, 9, 10, 11), (0,)),
        ((12, 13, 14, 15), (1, 2, 3)),
        ((), (4, 5)),
    ]
    last_near = tuple(range(6, leaves))
    state = dict(leaf=gram, node=heads, near=None)
    near_shape = shape((leaves, fan, slots, slots), bf16)

    def near_extras(near, operands, outs, scratch, aliases):
        operands += [("ids", neighbours, smem), ("own", own, vmem), ("low", low, vmem)]
        operands += [("high", high, vmem), ("columns", columns, vmem)]
        outs.append(("near_out", near_shape, anywhere))
        scratch.append(("tiles", pltpu.VMEM((len(near), fan, slots, slots), bf16)))
        scratch.append(("wide", pltpu.VMEM((9 * leaves, WIDTH), f32)))
        if state["near"] is not None:
            operands.append(("near_in", state["near"], anywhere))
            aliases["near_in"] = "near_out"
    parts = []

    def work(n, after):
        steps, near = plan[n]
        aliases = {}
        final = n == len(plan) - 1
        operands = [("after", after, anywhere)]
        outs, scratch = [], []
        if steps:
            rows = shape((STEP * len(steps) * GROUP, WIDTH), f32)
            operands += [("leaf_in", state["leaf"], vmem), ("node_in", state["node"], vmem)]
            outs += [(kind, rows, vmem) for kind in ("leaf_r", "leaf_s", "node_r")]
            if steps[-1] + 1 < STEPS:
                outs += [("leaf_out", flat, vmem), ("node_out", flat, vmem)]
        if n == 0:
            operands.append(("message", message, vmem))
            outs.append(("own", coords_shape, vmem))
        if near:
            near_extras(near, operands, outs, scratch, aliases)
        if final:
            for k, part in enumerate(parts):
                operands += [(f"{kind}{k}", part[kind], vmem) for kind in ("leaf_r", "leaf_s", "node_r")]
            operands.append(("basis", basis, vmem))
            outs += [("leaf_factors", mats, anywhere), ("node_factors", mats, anywhere)]
            outs.append(("leaf_bases", shape((leaves * slots, WIDTH), bf16), anywhere))
            scratch += [("factors", pltpu.VMEM(mats.shape, f32)), ("nodes", pltpu.VMEM(mats.shape, f32))]
            scratch.append(("bases", pltpu.VMEM((leaves * slots, WIDTH), bf16)))
        if near or final:
            scratch.append(("sems", pltpu.SemaphoreType.DMA((3 * GROUP + leaves,))))
        made = call(
            work_kernel, operands, outs, scratch, aliases, 3, f"work{n}",
            steps=steps, near=near, final=len(parts) if final else 0,
        )
        state["near"] = made.get("near_out", state["near"])
        if steps:
            parts.append(made)
            state["leaf"], state["node"] = made.get("leaf_out"), made.get("node_out")
        return made

    weight = chosen = weight_own
    made = low = high = own = None
    for level in range(levels):
        span = 2 ** (level + 1)
        quarter = span // 4
        if level == 0:
            left, right = lax.ppermute(weight, both, [(i, i + 1) for i in range(0, count, 2)]), weight
        else:
            first = [(i + quarter, i + 2 * quarter) for i in range(0, count, span)]
            second = [(i + 3 * quarter, i + 2 * quarter) for i in range(0, count, span)]
            if level + 1 == levels:
                first.append((3 * quarter, 0))
                second.append((quarter, 0))
            left, right = lax.ppermute(weight, both, first), lax.ppermute(weight, both, second)
        if level < len(plan):
            made = work(level, weight)
        if level == 0:
            own = made["own"]
            up = [(i, i + 1) for i in range(count - 1)]
            low = lax.ppermute(own, both, up)
            high = lax.ppermute(own, both, [(target, source) for source, target in up])
        if level + 1 < levels:
            weight, chosen = pl.pallas_call(
                functools.partial(lift_kernel, level=level),
                out_shape=[mat, mat],
                in_specs=[vmem] * 4 + [anywhere],
                out_specs=[vmem] * 2,
                compiler_params=params,
                cost_estimate=cost(0.4),
                name=f"lift{level}",
            )(left, right, move, chosen, next(iter(made.values())))

    operands = [
        ("left", left, vmem), ("right", right, vmem), ("chosen", chosen, vmem),
        ("node_in", made["node_factors"], anywhere),
    ]
    outs = [("node_out", mats, anywhere)]
    scratch = [("factor", pltpu.VMEM((WIDTH, WIDTH), f32)), ("sems", pltpu.SemaphoreType.DMA((leaves + 1,)))]
    aliases = {"node_in": "node_out"}
    near_extras(last_near, operands, outs, scratch, aliases)
    top = call(top_kernel, operands, outs, scratch, aliases, 6, "top", near=last_near, half=half)
    return (top["near_out"], made["leaf_bases"], made["leaf_factors"], top["node_out"])


def solution(mesh):
    both = ("grp", "dev")
    in_specs = (
        P(None, both),
        P(both),
        P(None, both),
        P(None, both),
        P(both, None, None),
        P(both, None, None),
    )
    out_specs = (
        P(both, None, None, None),
        P(both, None),
        P(both, None, None),
        P(both, None, None),
    )
    return jax.shard_map(shards, mesh=mesh, in_specs=in_specs, out_specs=out_specs, check_vma=False)
```

```python
import functools
import math

import jax
import jax.numpy as jnp
from jax import lax
from jax.experimental import pallas as pl
from jax.experimental.pallas import tpu as pltpu
from jax.sharding import PartitionSpec as P

ridge = 0.1
length_scale = 0.3
far = 1.0e6
f32 = jnp.float32
bf16 = jnp.bfloat16
STEP = 8
WIDTH = 128
GROUP = 8
STEPS = WIDTH // STEP
params = pltpu.CompilerParams(vmem_limit_bytes=40 * 1024 * 1024)
vmem = pl.BlockSpec(memory_space=pltpu.VMEM)
smem = pl.BlockSpec(memory_space=pltpu.SMEM)
anywhere = pl.BlockSpec(memory_space=pl.ANY)


def cost(micros):
    return pl.CostEstimate(flops=int(micros * 1.0e9), bytes_accessed=int(micros * 3.0e6), transcendentals=0)


def iota(shape, dim):
    return lax.broadcasted_iota(jnp.int32, shape, dim)


def split(value):
    high = value.astype(bf16)
    return high, (value - high.astype(f32)).astype(bf16)


def product(left, right, left_dim, right_dim):
    def dot(a, b):
        return lax.dot_general(a, b, (((left_dim,), (right_dim,)), ((), ())), preferred_element_type=f32)

    (lh, ll), (rh, rl) = split(left), split(right)
    return dot(lh, rh) + (dot(lh, rl) + dot(ll, rh))


def lift(move, head):
    return product(move, product(head, move, 1, 0), 0, 0)


def unit(scale):
    shape = (WIDTH, WIDTH)
    return jnp.where(iota(shape, 0) == iota(shape, 1), scale, 0.0).astype(f32)


def matern(delta_x, delta_y, delta_z):
    scale = 3.0**0.5 / length_scale * math.log2(math.e)
    square = delta_x * delta_x + delta_y * delta_y + delta_z * delta_z
    square = jnp.maximum(square * (scale * scale), 1e-30)
    u = square * lax.rsqrt(square)
    return (1.0 + u * math.log(2.0)) * jnp.exp2(-u)


def lane_copies(vreg, lane):
    return jnp.broadcast_to(vreg[:, lane : lane + 1], vreg.shape)


def add_up(terms):
    while len(terms) > 1:
        terms = [
            terms[a] + terms[a + 1] if a + 1 < len(terms) else terms[a] for a in range(0, len(terms), 2)
        ]
    return terms[0]


def rows_of(ref, i):
    return ref[GROUP * i : GROUP * (i + 1), :]


def stacked(ref, matrix):
    return ref[pl.ds(matrix, ref.shape[0] // GROUP, stride=GROUP), :]


def eliminate(s, get, put, put_r, put_s):
    at = STEP * s
    lane = iota((GROUP, WIDTH), 1)
    pivots = [get(at + i) for i in range(STEP)]
    cols = [[lane_copies(pivots[i], at + k) for k in range(i + 1)] for i in range(STEP)]
    spot = (lane >= at) & (lane < at + STEP)
    low = [[None] * STEP for _ in range(STEP)]
    inv = [None] * STEP
    made = [None] * STEP
    made_s = [None] * STEP
    for i in range(STEP):
        for k in range(i):
            t = cols[i][k]
            for m in range(k):
                t = t - low[i][m] * low[k][m]
            low[i][k] = t * inv[k]
        t = cols[i][i]
        for m in range(i):
            t = t - low[i][m] * low[i][m]
        inv[i] = lax.rsqrt(t)
        u = pivots[i]
        for m in range(i):
            u = u - low[i][m] * made[m]
        made[i] = u * inv[i]
        put_r(at + i, made[i])
        if put_s:
            u = jnp.where(spot, jnp.where(lane == at + i, 1.0, 0.0).astype(f32), pivots[i])
            for m in range(i):
                u = u - low[i][m] * made_s[m]
            made_s[i] = u * inv[i]
            put_s(at + i, made_s[i])
    first = at + STEP
    if first == WIDTH:
        return
    back = [None] * STEP
    for i in reversed(range(STEP)):
        t = (made_s if put_s else made)[i]
        for m in range(i + 1, STEP):
            t = t - low[m][i] * back[m]
        back[i] = t * inv[i]

    def start(i):
        return jnp.where(spot, 0.0, get(i)) if put_s else get(i)

    later = first + STEP
    for i in range(first, later):
        row = get(i)
        put(i, start(i) - add_up([lane_copies(row, at + k) * back[k] for k in range(STEP)]))
    if later == WIDTH:
        return
    index = at + (lane % 64) // GROUP
    own = lane % GROUP == iota((GROUP, WIDTH), 0)
    left = []
    for i in range(later, WIDTH):
        value = jnp.take_along_axis(get(i), index, axis=1, mode="promise_in_bounds")
        value = jnp.where(own, value, 0.0)
        high = value.astype(bf16).astype(f32)
        left.append(jnp.where(lane < 64, high, value - high))
    left = jnp.concatenate(left, axis=0).astype(bf16)
    right = jnp.concatenate(split(jnp.concatenate(back, axis=0)), axis=1)
    right = jnp.concatenate([right, right], axis=0)
    out = lax.dot_general(left, right, (((1,), (0,)), ((), ())), preferred_element_type=f32)
    out = out[:, :WIDTH] + out[:, WIDTH:]
    for i in range(later, WIDTH):
        put(i, start(i) - out[GROUP * (i - later) : GROUP * (i - later + 1), :])


def position():
    return lax.axis_index("grp") * lax.axis_size("dev") + lax.axis_index("dev")


def local_kernel(
    counts_in, coords_in, proxies_in, leaf_in, node_in,
    basis_ref, gram_ref, heads_ref, message_ref, move_ref, columns_ref,
    counts, coords, proxies, leaf_t, node_t, sems,
):
    pairs = ((counts_in, counts), (coords_in, coords), (proxies_in, proxies), (leaf_in, leaf_t), (node_in, node_t))
    copies = [pltpu.make_async_copy(a, b, sems.at[i]) for i, (a, b) in enumerate(pairs)]
    for copy in copies:
        copy.start()
    leaves = basis_ref.shape[0]
    eye = unit(ridge)
    shape = (WIDTH, WIDTH)
    for copy in copies[:3]:
        copy.wait()
    grams = []
    lane = iota((1, WIDTH), 1)
    for leaf in range(leaves):
        span = slice(leaf * WIDTH, leaf * WIDTH + WIDTH)
        own = coords[:, span]
        valid = lane < counts[leaf]
        at = WIDTH + 3 * leaf
        message_ref[at : at + 1, :] = jnp.where(valid, own[0:1], -far)
        message_ref[at + 1 : at + 3, :] = own[1:3]
        turned = jnp.concatenate([jnp.where(valid, own[0:1], far), own[1:3], jnp.zeros((5, WIDTH), f32)], axis=0).T
        side = [jnp.broadcast_to(turned[:, d : d + 1], shape) for d in range(3)]
        for d in range(3):
            columns_ref[leaf, d] = side[d]
        basis = matern(*(side[d] - jnp.broadcast_to(proxies[d : d + 1, span], shape) for d in range(3)))
        basis_ref[leaf] = basis
        gram = product(basis, basis, 0, 0) * (1.0 / WIDTH) + eye
        gram_ref[pl.ds(leaf, WIDTH, stride=GROUP), :] = gram
        grams.append(gram)
    copies[3].wait()
    weights = [lift(leaf_t[leaf], grams[leaf]) for leaf in range(leaves)]
    copies[4].wait()
    move_ref[...] = node_t[0]
    heads_ref[pl.ds(GROUP - 1, WIDTH, stride=GROUP), :] = eye
    at = 0
    level = 1
    while len(weights) > 1:
        following = []
        for k in range(len(weights) // 2):
            head = weights[2 * k] + weights[2 * k + 1] + eye
            heads_ref[pl.ds(at, WIDTH, stride=GROUP), :] = head
            at += 1
            following.append(lift(node_t[k * 2**level + 2 ** (level - 1)], head))
        weights = following
        level += 1
    message_ref[0:WIDTH, :] = weights[0]


def lift_kernel(left, right, move, chosen_in, token, weight_ref, chosen_ref, *, level):
    del token
    span = slice(0, WIDTH)
    head = left[span, :] + right[span, :] + unit(ridge)
    mine = position() % (2 ** (level + 1)) == 2**level
    chosen_ref[...] = jnp.where(mine, head, chosen_in[span, :])
    weight_ref[...] = lift(move[...], head)


def node_slots():
    slots = []
    level = 1
    while 2**level <= GROUP:
        slots += [k * 2**level + 2 ** (level - 1) for k in range(GROUP // 2**level)]
        level += 1
    return slots


class Copies:
    def __init__(self, sems):
        self.sems, self.made = sems, []

    def start(self, source, target):
        copy = pltpu.make_async_copy(source, target, self.sems.at[len(self.made)])
        copy.start()
        self.made.append(copy)

    def wait(self):
        for copy in self.made:
            copy.wait()


def near_tiles(ref, near, flush, copies):
    for n, leaf in enumerate(flush):
        copies.start(ref["tiles_in"].at[n], ref["near_out"].at[leaf])
    if not near:
        return None, 0
    ids, columns, wide = ref["ids"], ref["columns"], ref["wide"]
    leaves, fan = ids.shape[1], ids.shape[0]
    size = ref["swapped"].shape[0]
    odd = position() % 2 == 1
    first, own, second = (ref[n][-size:, :] for n in ("pair", "own", "swapped"))
    wide[0:size, :] = jnp.where(odd, first, second)
    wide[size : 2 * size, :] = own
    wide[2 * size : 3 * size, :] = jnp.where(odd, second, first)
    offset = (position() - 1) * leaves
    total = len(near) * fan
    later = "tiles_out" in ref
    tiles = ref["tiles_out" if later else "tiles"]

    def tile(t):
        at, n = divmod(t, fan)
        leaf = near[at]
        other = wide[pl.ds(3 * (ids[n, leaf] - offset), 3), :]
        shape = (WIDTH, WIDTH)
        value = matern(*(columns[leaf, d] - jnp.broadcast_to(other[d : d + 1], shape) for d in range(3)))
        tiles[at, n] = value.astype(bf16)
        if n == fan - 1 and not later:
            copies.start(tiles.at[at], ref["near_out"].at[leaf])

    return tile, total


def work_kernel(*refs, names, steps, near, flush, final):
    ref = dict(zip(names, refs))
    held = ({}, {})
    copies = Copies(ref["sems"]) if "sems" in ref else None
    tile, total = near_tiles(ref, near, flush, copies)
    done = 0
    share = -(-total // max(1, len(steps) - 1)) if steps else total
    for s in steps:
        for side, name in enumerate(("leaf", "node")):
            source, values = ref[name + "_in"], held[side]
            base = STEP * steps[0]

            def get(i, source=source, values=values):
                return values[i] if i in values else rows_of(source, i)

            def put(i, value, values=values):
                values[i] = value

            def store(kind):
                target = ref[kind]

                def put_row(i, value):
                    target[GROUP * (i - base) : GROUP * (i - base + 1), :] = value

                return put_row

            eliminate(s, get, put, store(name + "_r"), store("leaf_s") if name == "leaf" else None)
            if side == 0:
                for t in range(done, min(done + share, total)):
                    tile(t)
                done += share
    for side, name in enumerate(("leaf", "node")):
        if name + "_out" in ref:
            for i in range(STEP * (steps[-1] + 1), WIDTH):
                ref[name + "_out"][GROUP * i : GROUP * (i + 1), :] = held[side][i]
    if "coords_out" in ref:
        ref["coords_out"][...] = ref["message"][WIDTH:, :]
    if not final:
        if copies:
            copies.wait()
        return
    if not steps:
        for t in range(total):
            tile(t)
    parts = {kind: [ref[f"{kind}{n}"] for n in range(final)] for kind in ("leaf_r", "leaf_s", "node_r")}
    upper = iota((WIDTH, WIDTH), 1) >= iota((WIDTH, WIDTH), 0)
    lower = iota((WIDTH, WIDTH), 1) <= iota((WIDTH, WIDTH), 0)

    def whole(kind, b):
        return jnp.concatenate([stacked(part, b) for part in parts[kind]], axis=0)

    for b in range(GROUP):
        ref["factors"][b] = jnp.where(upper, whole("leaf_r", b), 0.0)
        copies.start(ref["factors"].at[b], ref["leaf_factors"].at[b])
        if b < GROUP - 1:
            ref["nodes"][b] = jnp.where(upper, whole("node_r", b), 0.0)
            copies.start(ref["nodes"].at[b], ref["node_factors"].at[node_slots()[b]])
    for b in range(GROUP):
        span = pl.ds(b * WIDTH, WIDTH)
        turned = jnp.where(lower, whole("leaf_s", b), 0.0)
        ref["bases"][span, :] = product(ref["basis"][b], turned, 1, 1).astype(bf16)
        copies.start(ref["bases"].at[span, :], ref["leaf_bases"].at[span, :])
    copies.wait()


def top_kernel(*refs, names, near, flush, half):
    ref = dict(zip(names, refs))
    copies = Copies(ref["sems"])
    tile, total = near_tiles(ref, near, flush, copies)
    left, right, chosen = ref["left"], ref["right"], ref["chosen"]
    top = jnp.where(position() % half == 0, left[...] + right[...] + unit(ridge), chosen[...])
    values = {}

    def get(i):
        return values[i] if i in values else jnp.broadcast_to(top[i : i + 1, :], (GROUP, WIDTH))

    def put(i, value):
        values[i] = value

    lane = iota((1, WIDTH), 1)
    target = ref["factor"]

    def put_r(i, value):
        target[i : i + 1, :] = jnp.where(lane >= i, value[0:1, :], 0.0)

    share = -(-total // (STEPS - 4))
    for s in range(STEPS):
        eliminate(s, get, put, put_r, None)
        for t in range(s * share, min((s + 1) * share, total)):
            tile(t)
    copies.start(target, ref["node_out"].at[0])
    copies.wait()


def call(body, operands, outs, scratch, aliases, micros, name, **static):
    names = [o[0] for o in operands] + [o[0] for o in outs] + [s[0] for s in scratch]
    at = {o[0]: n for n, o in enumerate(operands)}
    to = {o[0]: n for n, o in enumerate(outs)}
    made = pl.pallas_call(
        functools.partial(body, names=names, **static),
        out_shape=[o[1] for o in outs],
        in_specs=[o[2] for o in operands],
        out_specs=[o[2] for o in outs],
        scratch_shapes=[s[1] for s in scratch],
        input_output_aliases={at[a]: to[b] for a, b in aliases.items()},
        compiler_params=params,
        cost_estimate=cost(micros),
        name=name,
    )(*(o[1] for o in operands))
    return dict(zip(to, made))


def shards(coords, counts, neighbours, proxies, leaf_transfers, node_transfers):
    leaves = counts.shape[0]
    slots = coords.shape[1] // leaves
    fan = neighbours.shape[0]
    count = lax.axis_size("grp") * lax.axis_size("dev")
    levels = count.bit_length() - 1
    half = count // 2
    both = ("grp", "dev")
    shape = jax.ShapeDtypeStruct
    mat = shape((WIDTH, WIDTH), f32)
    mats = shape((leaves, WIDTH, WIDTH), f32)
    flat = shape((WIDTH * GROUP, WIDTH), f32)
    coords_shape = shape((3 * leaves, WIDTH), f32)
    long = shape((WIDTH + 3 * leaves, WIDTH), f32)

    basis, gram, heads, message, move, columns = pl.pallas_call(
        local_kernel,
        out_shape=(mats, flat, flat, long, mat, shape((leaves, 3, slots, WIDTH), f32)),
        in_specs=[anywhere] * 5,
        out_specs=(vmem,) * 6,
        scratch_shapes=[
            pltpu.SMEM(counts.shape, jnp.int32),
            pltpu.VMEM(coords.shape, f32),
            pltpu.VMEM(proxies.shape, f32),
            pltpu.VMEM(leaf_transfers.shape, f32),
            pltpu.VMEM(node_transfers.shape, f32),
            pltpu.SemaphoreType.DMA((5,)),
        ],
        compiler_params=params,
        cost_estimate=cost(4),
        name="local",
    )(*(pltpu.with_memory_space_constraint(x, pltpu.HBM) for x in (counts, coords, proxies, leaf_transfers, node_transfers)))

    plan = [
        ((0, 1, 2, 3), ()),
        ((4, 5, 6, 7), ()),
        ((8, 9, 10, 11), ()),
        ((12, 13, 14, 15), (0, 1, 2)),
        ((), (3, 4, 5)),
    ]
    parts = []
    last_near = tuple(range(6, leaves))
    state = dict(leaf=gram, node=heads, near=None, tiles=None, flush=())

    def near_extras(near, flush, later, operands, outs, scratch, aliases):
        if near:
            operands += [("ids", neighbours, smem), ("own", message, vmem), ("pair", pair, vmem)]
            operands += [("swapped", swapped, vmem), ("columns", columns, vmem)]
            scratch.append(("wide", pltpu.VMEM((9 * leaves, WIDTH), f32)))
            tiles = (len(near), fan, slots, slots)
            if later:
                outs.append(("tiles_out", shape(tiles, bf16), vmem))
            else:
                scratch.append(("tiles", pltpu.VMEM(tiles, bf16)))
        if flush:
            operands.append(("tiles_in", state["tiles"], vmem))
        if flush or (near and not later):
            outs.append(("near_out", shape((leaves, fan, slots, slots), bf16), anywhere))
            if state["near"] is not None:
                operands.append(("near_in", state["near"], anywhere))
                aliases["near_in"] = "near_out"

    def work(n, after):
        steps, near = plan[n]
        aliases = {}
        final = n == len(plan) - 1
        operands = [("after", after, anywhere)]
        outs, scratch = [], []
        if steps:
            rows = shape((STEP * len(steps) * GROUP, WIDTH), f32)
            operands += [("leaf_in", state["leaf"], vmem), ("node_in", state["node"], vmem)]
            outs += [(kind, rows, vmem) for kind in ("leaf_r", "leaf_s", "node_r")]
            if steps[-1] + 1 < STEPS:
                outs += [("leaf_out", flat, vmem), ("node_out", flat, vmem)]
        if n == 1:
            operands.append(("message", message, vmem))
            outs.append(("coords_out", coords_shape, vmem))
        flush = state["flush"]
        near_extras(near, flush, True, operands, outs, scratch, aliases)
        if final:
            for k, part in enumerate(parts):
                operands += [(f"{kind}{k}", part[kind], vmem) for kind in ("leaf_r", "leaf_s", "node_r")]
            operands.append(("basis", basis, vmem))
            outs += [("leaf_factors", mats, anywhere), ("node_factors", mats, anywhere)]
            outs.append(("leaf_bases", shape((leaves * slots, WIDTH), bf16), anywhere))
            scratch += [("factors", pltpu.VMEM(mats.shape, f32)), ("nodes", pltpu.VMEM(mats.shape, f32))]
            scratch.append(("bases", pltpu.VMEM((leaves * slots, WIDTH), bf16)))
        if flush or final:
            scratch.append(("sems", pltpu.SemaphoreType.DMA((3 * GROUP + leaves,))))
        made = call(
            work_kernel, operands, outs, scratch, aliases, 3, f"work{n}",
            steps=steps, near=near, flush=flush, final=len(parts) if final else 0,
        )
        state["near"] = made.get("near_out", state["near"])
        state["tiles"], state["flush"] = made.get("tiles_out"), near
        if steps:
            parts.append(made)
            state["leaf"], state["node"] = made.get("leaf_out"), made.get("node_out")
        return made

    weight = chosen = message
    made = pair = swapped = None
    for level in range(levels):
        span = 2 ** (level + 1)
        quarter = span // 4
        if level == 0:
            pair = lax.ppermute(weight, both, [(i, i ^ 1) for i in range(count)])
            left, right = pair, weight
        else:
            first = [(i + quarter, i + 2 * quarter) for i in range(0, count, span)]
            second = [(i + 3 * quarter, i + 2 * quarter) for i in range(0, count, span)]
            if level + 1 == levels:
                first.append((3 * quarter, 0))
                second.append((quarter, 0))
            left, right = lax.ppermute(weight, both, first), lax.ppermute(weight, both, second)
        if level < len(plan):
            made = work(level, weight)
        if level == 1:
            others = [(i, i + 1) for i in range(1, count - 1, 2)]
            others += [(target, source) for source, target in others]
            swapped = lax.ppermute(made["coords_out"], both, others)
        if level + 1 < levels:
            weight, chosen = pl.pallas_call(
                functools.partial(lift_kernel, level=level),
                out_shape=[mat, mat],
                in_specs=[vmem] * 4 + [anywhere],
                out_specs=[vmem] * 2,
                compiler_params=params,
                cost_estimate=cost(0.4),
                name=f"lift{level}",
            )(left, right, move, chosen, next(iter(made.values())))

    operands = [
        ("left", left, vmem), ("right", right, vmem), ("chosen", chosen, vmem),
        ("node_in", made["node_factors"], anywhere),
    ]
    outs = [("node_out", mats, anywhere)]
    scratch = [("factor", pltpu.VMEM((WIDTH, WIDTH), f32)), ("sems", pltpu.SemaphoreType.DMA((leaves + 1,)))]
    aliases = {"node_in": "node_out"}
    near_extras(last_near, state["flush"], False, operands, outs, scratch, aliases)
    top = call(
        top_kernel, operands, outs, scratch, aliases, 6, "top", near=last_near, flush=state["flush"], half=half
    )
    return (top["near_out"], made["leaf_bases"], made["leaf_factors"], top["node_out"])


def solution(mesh):
    both = ("grp", "dev")
    in_specs = (
        P(None, both),
        P(both),
        P(None, both),
        P(None, both),
        P(both, None, None),
        P(both, None, None),
    )
    out_specs = (
        P(both, None, None, None),
        P(both, None),
        P(both, None, None),
        P(both, None, None),
    )
    return jax.shard_map(shards, mesh=mesh, in_specs=in_specs, out_specs=out_specs, check_vma=False)
```

```python
import functools
import math

import jax
import jax.numpy as jnp
from jax import lax
from jax.experimental import pallas as pl
from jax.experimental.pallas import tpu as pltpu
from jax.sharding import PartitionSpec as P

ridge = 0.1
length_scale = 0.3
far = 1.0e6
f32 = jnp.float32
bf16 = jnp.bfloat16
STEP = 8
WIDTH = 128
GROUP = 8
STEPS = WIDTH // STEP
params = pltpu.CompilerParams(vmem_limit_bytes=40 * 1024 * 1024)
vmem = pl.BlockSpec(memory_space=pltpu.VMEM)
smem = pl.BlockSpec(memory_space=pltpu.SMEM)
anywhere = pl.BlockSpec(memory_space=pl.ANY)


def cost(micros):
    return pl.CostEstimate(flops=int(micros * 1.0e9), bytes_accessed=int(micros * 3.0e6), transcendentals=0)


def iota(shape, dim):
    return lax.broadcasted_iota(jnp.int32, shape, dim)


def split(value):
    high = value.astype(bf16)
    return high, (value - high.astype(f32)).astype(bf16)


def product(left, right, left_dim, right_dim):
    def dot(a, b):
        return lax.dot_general(a, b, (((left_dim,), (right_dim,)), ((), ())), preferred_element_type=f32)

    (lh, ll), (rh, rl) = split(left), split(right)
    return dot(lh, rh) + (dot(lh, rl) + dot(ll, rh))


def lift(move, head):
    return product(move, product(head, move, 1, 0), 0, 0)


def unit(scale):
    shape = (WIDTH, WIDTH)
    return jnp.where(iota(shape, 0) == iota(shape, 1), scale, 0.0).astype(f32)


def matern(delta_x, delta_y, delta_z):
    scale = 3.0**0.5 / length_scale * math.log2(math.e)
    square = delta_x * delta_x + delta_y * delta_y + delta_z * delta_z
    square = jnp.maximum(square * (scale * scale), 1e-30)
    u = square * lax.rsqrt(square)
    return (1.0 + u * math.log(2.0)) * jnp.exp2(-u)


def lane_copies(vreg, lane):
    return jnp.broadcast_to(vreg[:, lane : lane + 1], vreg.shape)


def add_up(terms):
    while len(terms) > 1:
        terms = [
            terms[a] + terms[a + 1] if a + 1 < len(terms) else terms[a] for a in range(0, len(terms), 2)
        ]
    return terms[0]


def rows_of(ref, i):
    return ref[GROUP * i : GROUP * (i + 1), :]


def stacked(ref, matrix):
    return ref[pl.ds(matrix, ref.shape[0] // GROUP, stride=GROUP), :]


def eliminate(s, get, put, put_r, put_s):
    at = STEP * s
    lane = iota((GROUP, WIDTH), 1)
    pivots = [get(at + i) for i in range(STEP)]
    cols = [[lane_copies(pivots[i], at + k) for k in range(i + 1)] for i in range(STEP)]
    spot = (lane >= at) & (lane < at + STEP)
    low = [[None] * STEP for _ in range(STEP)]
    inv = [None] * STEP
    made = [None] * STEP
    made_s = [None] * STEP
    for i in range(STEP):
        for k in range(i):
            t = cols[i][k]
            for m in range(k):
                t = t - low[i][m] * low[k][m]
            low[i][k] = t * inv[k]
        t = cols[i][i]
        for m in range(i):
            t = t - low[i][m] * low[i][m]
        inv[i] = lax.rsqrt(t)
        u = pivots[i]
        for m in range(i):
            u = u - low[i][m] * made[m]
        made[i] = u * inv[i]
        put_r(at + i, made[i])
        if put_s:
            u = jnp.where(spot, jnp.where(lane == at + i, 1.0, 0.0).astype(f32), pivots[i])
            for m in range(i):
                u = u - low[i][m] * made_s[m]
            made_s[i] = u * inv[i]
            put_s(at + i, made_s[i])
    first = at + STEP
    if first == WIDTH:
        return
    back = [None] * STEP
    for i in reversed(range(STEP)):
        t = (made_s if put_s else made)[i]
        for m in range(i + 1, STEP):
            t = t - low[m][i] * back[m]
        back[i] = t * inv[i]

    def start(i):
        return jnp.where(spot, 0.0, get(i)) if put_s else get(i)

    later = first + STEP
    for i in range(first, later):
        row = get(i)
        put(i, start(i) - add_up([lane_copies(row, at + k) * back[k] for k in range(STEP)]))
    if later == WIDTH:
        return
    index = at + (lane % 64) // GROUP
    own = lane % GROUP == iota((GROUP, WIDTH), 0)
    left = []
    for i in range(later, WIDTH):
        value = jnp.take_along_axis(get(i), index, axis=1, mode="promise_in_bounds")
        value = jnp.where(own, value, 0.0)
        high = value.astype(bf16).astype(f32)
        left.append(jnp.where(lane < 64, high, value - high))
    left = jnp.concatenate(left, axis=0).astype(bf16)
    right = jnp.concatenate(split(jnp.concatenate(back, axis=0)), axis=1)
    right = jnp.concatenate([right, right], axis=0)
    out = lax.dot_general(left, right, (((1,), (0,)), ((), ())), preferred_element_type=f32)
    out = out[:, :WIDTH] + out[:, WIDTH:]
    for i in range(later, WIDTH):
        put(i, start(i) - out[GROUP * (i - later) : GROUP * (i - later + 1), :])


def position():
    return lax.axis_index("grp") * lax.axis_size("dev") + lax.axis_index("dev")


def local_kernel(
    counts_in, coords_in, proxies_in, leaf_in, node_in,
    basis_ref, gram_ref, heads_ref, message_ref, move_ref, columns_ref, coords_ref,
    counts, coords, proxies, leaf_t, node_t, sems,
):
    pairs = ((counts_in, counts), (coords_in, coords), (proxies_in, proxies), (leaf_in, leaf_t), (node_in, node_t))
    copies = [pltpu.make_async_copy(a, b, sems.at[i]) for i, (a, b) in enumerate(pairs)]
    for copy in copies:
        copy.start()
    leaves = basis_ref.shape[0]
    eye = unit(ridge)
    shape = (WIDTH, WIDTH)
    for copy in copies[:3]:
        copy.wait()
    grams = []
    lane = iota((1, WIDTH), 1)
    for leaf in range(leaves):
        span = slice(leaf * WIDTH, leaf * WIDTH + WIDTH)
        own = coords[:, span]
        valid = lane < counts[leaf]
        at = WIDTH + 3 * leaf
        message_ref[at : at + 1, :] = jnp.where(valid, own[0:1], -far)
        message_ref[at + 1 : at + 3, :] = own[1:3]
        turned = jnp.concatenate([jnp.where(valid, own[0:1], far), own[1:3], jnp.zeros((5, WIDTH), f32)], axis=0).T
        side = [jnp.broadcast_to(turned[:, d : d + 1], shape) for d in range(3)]
        for d in range(3):
            columns_ref[leaf, d] = side[d]
        basis = matern(*(side[d] - jnp.broadcast_to(proxies[d : d + 1, span], shape) for d in range(3)))
        basis_ref[leaf] = basis
        gram = product(basis, basis, 0, 0) * (1.0 / WIDTH) + eye
        gram_ref[pl.ds(leaf, WIDTH, stride=GROUP), :] = gram
        grams.append(gram)
    copies[3].wait()
    weights = [lift(leaf_t[leaf], grams[leaf]) for leaf in range(leaves)]
    copies[4].wait()
    move_ref[...] = node_t[0]
    heads_ref[pl.ds(GROUP - 1, WIDTH, stride=GROUP), :] = eye
    at = 0
    level = 1
    while len(weights) > 1:
        following = []
        for k in range(len(weights) // 2):
            head = weights[2 * k] + weights[2 * k + 1] + eye
            heads_ref[pl.ds(at, WIDTH, stride=GROUP), :] = head
            at += 1
            following.append(lift(node_t[k * 2**level + 2 ** (level - 1)], head))
        weights = following
        level += 1
    message_ref[0:WIDTH, :] = weights[0]
    coords_ref[...] = message_ref[WIDTH:, :]


def lift_kernel(left, right, move, chosen_in, token, weight_ref, chosen_ref, *, level):
    del token
    span = slice(0, WIDTH)
    head = left[span, :] + right[span, :] + unit(ridge)
    mine = position() % (2 ** (level + 1)) == 2**level
    chosen_ref[...] = jnp.where(mine, head, chosen_in[span, :])
    weight_ref[...] = lift(move[...], head)


def node_slots():
    slots = []
    level = 1
    while 2**level <= GROUP:
        slots += [k * 2**level + 2 ** (level - 1) for k in range(GROUP // 2**level)]
        level += 1
    return slots


class Copies:
    def __init__(self, sems):
        self.sems, self.made = sems, []

    def start(self, source, target):
        copy = pltpu.make_async_copy(source, target, self.sems.at[len(self.made)])
        copy.start()
        self.made.append(copy)

    def wait(self):
        for copy in self.made:
            copy.wait()


def near_tiles(ref, near, flush, copies):
    for n, leaf in enumerate(flush):
        copies.start(ref["tiles_in"].at[n], ref["near_out"].at[leaf])
    if not near:
        return None, 0
    ids, columns, wide = ref["ids"], ref["columns"], ref["wide"]
    leaves, fan = ids.shape[1], ids.shape[0]
    size = ref["swapped"].shape[0]
    odd = position() % 2 == 1
    first, own, second = (ref[n][-size:, :] for n in ("pair", "own", "swapped"))
    wide[0:size, :] = jnp.where(odd, first, second)
    wide[size : 2 * size, :] = own
    wide[2 * size : 3 * size, :] = jnp.where(odd, second, first)
    offset = (position() - 1) * leaves
    total = len(near) * fan
    later = "tiles_out" in ref
    tiles = ref["tiles_out" if later else "tiles"]

    def tile(t):
        at, n = divmod(t, fan)
        leaf = near[at]
        other = wide[pl.ds(3 * (ids[n, leaf] - offset), 3), :]
        shape = (WIDTH, WIDTH)
        value = matern(*(columns[leaf, d] - jnp.broadcast_to(other[d : d + 1], shape) for d in range(3)))
        tiles[at, n] = value.astype(bf16)
        if n == fan - 1 and not later:
            copies.start(tiles.at[at], ref["near_out"].at[leaf])

    return tile, total


def work_kernel(*refs, names, steps, near, flush, final):
    ref = dict(zip(names, refs))
    held = ({}, {})
    copies = Copies(ref["sems"]) if "sems" in ref else None
    tile, total = near_tiles(ref, near, flush, copies)
    done = 0
    share = -(-total // max(1, len(steps) - 1)) if steps else total
    for s in steps:
        for side, name in enumerate(("leaf", "node")):
            source, values = ref[name + "_in"], held[side]
            base = STEP * steps[0]

            def get(i, source=source, values=values):
                return values[i] if i in values else rows_of(source, i)

            def put(i, value, values=values):
                values[i] = value

            def store(kind):
                target = ref[kind]

                def put_row(i, value):
                    target[GROUP * (i - base) : GROUP * (i - base + 1), :] = value

                return put_row

            eliminate(s, get, put, store(name + "_r"), store("leaf_s") if name == "leaf" else None)
            if side == 0:
                for t in range(done, min(done + share, total)):
                    tile(t)
                done += share
    for side, name in enumerate(("leaf", "node")):
        if name + "_out" in ref:
            for i in range(STEP * (steps[-1] + 1), WIDTH):
                ref[name + "_out"][GROUP * i : GROUP * (i + 1), :] = held[side][i]
    if "coords_out" in ref:
        ref["coords_out"][...] = ref["message"][WIDTH:, :]
    if not final:
        if copies:
            copies.wait()
        return
    if not steps:
        for t in range(total):
            tile(t)
    parts = {kind: [ref[f"{kind}{n}"] for n in range(final)] for kind in ("leaf_r", "leaf_s", "node_r")}
    upper = iota((WIDTH, WIDTH), 1) >= iota((WIDTH, WIDTH), 0)
    lower = iota((WIDTH, WIDTH), 1) <= iota((WIDTH, WIDTH), 0)

    def whole(kind, b):
        return jnp.concatenate([stacked(part, b) for part in parts[kind]], axis=0)

    for b in range(GROUP):
        ref["factors"][b] = jnp.where(upper, whole("leaf_r", b), 0.0)
        copies.start(ref["factors"].at[b], ref["leaf_factors"].at[b])
        if b < GROUP - 1:
            ref["nodes"][b] = jnp.where(upper, whole("node_r", b), 0.0)
            copies.start(ref["nodes"].at[b], ref["node_factors"].at[node_slots()[b]])
    for b in range(GROUP):
        span = pl.ds(b * WIDTH, WIDTH)
        turned = jnp.where(lower, whole("leaf_s", b), 0.0)
        ref["bases"][span, :] = product(ref["basis"][b], turned, 1, 1).astype(bf16)
        copies.start(ref["bases"].at[span, :], ref["leaf_bases"].at[span, :])
    copies.wait()


def top_kernel(*refs, names, near, flush, half):
    ref = dict(zip(names, refs))
    copies = Copies(ref["sems"])
    tile, total = near_tiles(ref, near, flush, copies)
    left, right, chosen = ref["left"], ref["right"], ref["chosen"]
    top = jnp.where(position() % half == 0, left[...] + right[...] + unit(ridge), chosen[...])
    values = {}

    def get(i):
        return values[i] if i in values else jnp.broadcast_to(top[i : i + 1, :], (GROUP, WIDTH))

    def put(i, value):
        values[i] = value

    lane = iota((1, WIDTH), 1)
    target = ref["factor"]

    def put_r(i, value):
        target[i : i + 1, :] = jnp.where(lane >= i, value[0:1, :], 0.0)

    share = -(-total // (STEPS - 4))
    for s in range(STEPS):
        eliminate(s, get, put, put_r, None)
        for t in range(s * share, min((s + 1) * share, total)):
            tile(t)
    copies.start(target, ref["node_out"].at[0])
    copies.wait()


def call(body, operands, outs, scratch, aliases, micros, name, **static):
    names = [o[0] for o in operands] + [o[0] for o in outs] + [s[0] for s in scratch]
    at = {o[0]: n for n, o in enumerate(operands)}
    to = {o[0]: n for n, o in enumerate(outs)}
    made = pl.pallas_call(
        functools.partial(body, names=names, **static),
        out_shape=[o[1] for o in outs],
        in_specs=[o[2] for o in operands],
        out_specs=[o[2] for o in outs],
        scratch_shapes=[s[1] for s in scratch],
        input_output_aliases={at[a]: to[b] for a, b in aliases.items()},
        compiler_params=params,
        cost_estimate=cost(micros),
        name=name,
    )(*(o[1] for o in operands))
    return dict(zip(to, made))


def shards(coords, counts, neighbours, proxies, leaf_transfers, node_transfers):
    leaves = counts.shape[0]
    slots = coords.shape[1] // leaves
    fan = neighbours.shape[0]
    count = lax.axis_size("grp") * lax.axis_size("dev")
    levels = count.bit_length() - 1
    half = count // 2
    both = ("grp", "dev")
    shape = jax.ShapeDtypeStruct
    mat = shape((WIDTH, WIDTH), f32)
    mats = shape((leaves, WIDTH, WIDTH), f32)
    flat = shape((WIDTH * GROUP, WIDTH), f32)
    coords_shape = shape((3 * leaves, WIDTH), f32)
    long = shape((WIDTH + 3 * leaves, WIDTH), f32)

    basis, gram, heads, message, move, columns, coords_own = pl.pallas_call(
        local_kernel,
        out_shape=(mats, flat, flat, long, mat, shape((leaves, 3, slots, WIDTH), f32), coords_shape),
        in_specs=[anywhere] * 5,
        out_specs=(vmem,) * 7,
        scratch_shapes=[
            pltpu.SMEM(counts.shape, jnp.int32),
            pltpu.VMEM(coords.shape, f32),
            pltpu.VMEM(proxies.shape, f32),
            pltpu.VMEM(leaf_transfers.shape, f32),
            pltpu.VMEM(node_transfers.shape, f32),
            pltpu.SemaphoreType.DMA((5,)),
        ],
        compiler_params=params,
        cost_estimate=cost(4),
        name="local",
    )(*(pltpu.with_memory_space_constraint(x, pltpu.HBM) for x in (counts, coords, proxies, leaf_transfers, node_transfers)))

    plan = [
        ((0, 1, 2, 3), ()),
        ((4, 5, 6, 7), ()),
        ((8, 9, 10, 11), ()),
        ((12, 13, 14, 15), (0, 1, 2)),
        ((), (3, 4, 5)),
    ]
    parts = []
    last_near = tuple(range(6, leaves))
    state = dict(leaf=gram, node=heads, near=None, tiles=None, flush=())

    def near_extras(near, flush, later, operands, outs, scratch, aliases):
        if near:
            operands += [("ids", neighbours, smem), ("own", message, vmem), ("pair", pair, vmem)]
            operands += [("swapped", swapped, vmem), ("columns", columns, vmem)]
            scratch.append(("wide", pltpu.VMEM((9 * leaves, WIDTH), f32)))
            tiles = (len(near), fan, slots, slots)
            if later:
                outs.append(("tiles_out", shape(tiles, bf16), vmem))
            else:
                scratch.append(("tiles", pltpu.VMEM(tiles, bf16)))
        if flush:
            operands.append(("tiles_in", state["tiles"], vmem))
        if flush or (near and not later):
            outs.append(("near_out", shape((leaves, fan, slots, slots), bf16), anywhere))
            if state["near"] is not None:
                operands.append(("near_in", state["near"], anywhere))
                aliases["near_in"] = "near_out"

    def work(n, after):
        steps, near = plan[n]
        aliases = {}
        final = n == len(plan) - 1
        operands = [("after", after, anywhere)]
        outs, scratch = [], []
        if steps:
            rows = shape((STEP * len(steps) * GROUP, WIDTH), f32)
            operands += [("leaf_in", state["leaf"], vmem), ("node_in", state["node"], vmem)]
            outs += [(kind, rows, vmem) for kind in ("leaf_r", "leaf_s", "node_r")]
            if steps[-1] + 1 < STEPS:
                outs += [("leaf_out", flat, vmem), ("node_out", flat, vmem)]
        flush = state["flush"]
        near_extras(near, flush, True, operands, outs, scratch, aliases)
        if final:
            for k, part in enumerate(parts):
                operands += [(f"{kind}{k}", part[kind], vmem) for kind in ("leaf_r", "leaf_s", "node_r")]
            operands.append(("basis", basis, vmem))
            outs += [("leaf_factors", mats, anywhere), ("node_factors", mats, anywhere)]
            outs.append(("leaf_bases", shape((leaves * slots, WIDTH), bf16), anywhere))
            scratch += [("factors", pltpu.VMEM(mats.shape, f32)), ("nodes", pltpu.VMEM(mats.shape, f32))]
            scratch.append(("bases", pltpu.VMEM((leaves * slots, WIDTH), bf16)))
        if flush or final:
            scratch.append(("sems", pltpu.SemaphoreType.DMA((3 * GROUP + leaves,))))
        made = call(
            work_kernel, operands, outs, scratch, aliases, 3, f"work{n}",
            steps=steps, near=near, flush=flush, final=len(parts) if final else 0,
        )
        state["near"] = made.get("near_out", state["near"])
        state["tiles"], state["flush"] = made.get("tiles_out"), near
        if steps:
            parts.append(made)
            state["leaf"], state["node"] = made.get("leaf_out"), made.get("node_out")
        return made

    weight = chosen = message
    made = pair = None
    others = [(i, i + 1) for i in range(1, count - 1, 2)]
    others += [(target, source) for source, target in others]
    swapped = lax.ppermute(coords_own, both, others)
    for level in range(levels):
        span = 2 ** (level + 1)
        quarter = span // 4
        if level == 0:
            pair = lax.ppermute(weight, both, [(i, i ^ 1) for i in range(count)])
            left, right = pair, weight
        else:
            first = [(i + quarter, i + 2 * quarter) for i in range(0, count, span)]
            second = [(i + 3 * quarter, i + 2 * quarter) for i in range(0, count, span)]
            if level + 1 == levels:
                first.append((3 * quarter, 0))
                second.append((quarter, 0))
            left, right = lax.ppermute(weight, both, first), lax.ppermute(weight, both, second)
        if level < len(plan):
            made = work(level, weight)
        if level + 1 < levels:
            weight, chosen = pl.pallas_call(
                functools.partial(lift_kernel, level=level),
                out_shape=[mat, mat],
                in_specs=[vmem] * 4 + [anywhere],
                out_specs=[vmem] * 2,
                compiler_params=params,
                cost_estimate=cost(0.4),
                name=f"lift{level}",
            )(left, right, move, chosen, next(iter(made.values())))

    operands = [
        ("left", left, vmem), ("right", right, vmem), ("chosen", chosen, vmem),
        ("node_in", made["node_factors"], anywhere),
    ]
    outs = [("node_out", mats, anywhere)]
    scratch = [("factor", pltpu.VMEM((WIDTH, WIDTH), f32)), ("sems", pltpu.SemaphoreType.DMA((leaves + 1,)))]
    aliases = {"node_in": "node_out"}
    near_extras(last_near, state["flush"], False, operands, outs, scratch, aliases)
    top = call(
        top_kernel, operands, outs, scratch, aliases, 6, "top", near=last_near, flush=state["flush"], half=half
    )
    return (top["near_out"], made["leaf_bases"], made["leaf_factors"], top["node_out"])


def solution(mesh):
    both = ("grp", "dev")
    in_specs = (
        P(None, both),
        P(both),
        P(None, both),
        P(None, both),
        P(both, None, None),
        P(both, None, None),
    )
    out_specs = (
        P(both, None, None, None),
        P(both, None),
        P(both, None, None),
        P(both, None, None),
    )
    return jax.shard_map(shards, mesh=mesh, in_specs=in_specs, out_specs=out_specs, check_vma=False)
```

```python
import functools
import math

import jax
import jax.numpy as jnp
from jax import lax
from jax.experimental import pallas as pl
from jax.experimental.pallas import tpu as pltpu
from jax.sharding import PartitionSpec as P

ridge = 0.1
length_scale = 0.3
far = 1.0e6
f32 = jnp.float32
bf16 = jnp.bfloat16
STEP = 8
WIDTH = 128
GROUP = 8
STEPS = WIDTH // STEP
params = pltpu.CompilerParams(vmem_limit_bytes=40 * 1024 * 1024)
vmem = pl.BlockSpec(memory_space=pltpu.VMEM)
smem = pl.BlockSpec(memory_space=pltpu.SMEM)
anywhere = pl.BlockSpec(memory_space=pl.ANY)


def cost(micros):
    return pl.CostEstimate(flops=int(micros * 1.0e9), bytes_accessed=int(micros * 3.0e6), transcendentals=0)


def iota(shape, dim):
    return lax.broadcasted_iota(jnp.int32, shape, dim)


def split(value):
    high = value.astype(bf16)
    return high, (value - high.astype(f32)).astype(bf16)


def product(left, right, left_dim, right_dim):
    def dot(a, b):
        return lax.dot_general(a, b, (((left_dim,), (right_dim,)), ((), ())), preferred_element_type=f32)

    (lh, ll), (rh, rl) = split(left), split(right)
    return dot(lh, rh) + (dot(lh, rl) + dot(ll, rh))


def lift(move, head):
    return product(move, product(head, move, 1, 0), 0, 0)


def unit(scale):
    shape = (WIDTH, WIDTH)
    return jnp.where(iota(shape, 0) == iota(shape, 1), scale, 0.0).astype(f32)


def matern(delta_x, delta_y, delta_z):
    scale = 3.0**0.5 / length_scale * math.log2(math.e)
    square = delta_x * delta_x + delta_y * delta_y + delta_z * delta_z
    square = jnp.maximum(square * (scale * scale), 1e-30)
    u = square * lax.rsqrt(square)
    return (1.0 + u * math.log(2.0)) * jnp.exp2(-u)


def lane_copies(vreg, lane):
    return jnp.broadcast_to(vreg[:, lane : lane + 1], vreg.shape)


def add_up(terms):
    while len(terms) > 1:
        terms = [
            terms[a] + terms[a + 1] if a + 1 < len(terms) else terms[a] for a in range(0, len(terms), 2)
        ]
    return terms[0]


def rows_of(ref, i):
    return ref[GROUP * i : GROUP * (i + 1), :]


def stacked(ref, matrix):
    return ref[pl.ds(matrix, ref.shape[0] // GROUP, stride=GROUP), :]


def eliminate(s, get, put, put_r, put_s):
    at = STEP * s
    lane = iota((GROUP, WIDTH), 1)
    pivots = [get(at + i) for i in range(STEP)]
    cols = [[lane_copies(pivots[i], at + k) for k in range(i + 1)] for i in range(STEP)]
    spot = (lane >= at) & (lane < at + STEP)
    low = [[None] * STEP for _ in range(STEP)]
    inv = [None] * STEP
    made = [None] * STEP
    made_s = [None] * STEP
    for i in range(STEP):
        for k in range(i):
            t = cols[i][k]
            for m in range(k):
                t = t - low[i][m] * low[k][m]
            low[i][k] = t * inv[k]
        t = cols[i][i]
        for m in range(i):
            t = t - low[i][m] * low[i][m]
        inv[i] = lax.rsqrt(t)
        u = pivots[i]
        for m in range(i):
            u = u - low[i][m] * made[m]
        made[i] = u * inv[i]
        put_r(at + i, made[i])
        if put_s:
            u = jnp.where(spot, jnp.where(lane == at + i, 1.0, 0.0).astype(f32), pivots[i])
            for m in range(i):
                u = u - low[i][m] * made_s[m]
            made_s[i] = u * inv[i]
            put_s(at + i, made_s[i])
    first = at + STEP
    if first == WIDTH:
        return
    back = [None] * STEP
    for i in reversed(range(STEP)):
        t = (made_s if put_s else made)[i]
        for m in range(i + 1, STEP):
            t = t - low[m][i] * back[m]
        back[i] = t * inv[i]

    def start(i):
        return jnp.where(spot, 0.0, get(i)) if put_s else get(i)

    later = first + STEP
    for i in range(first, later):
        row = get(i)
        put(i, start(i) - add_up([lane_copies(row, at + k) * back[k] for k in range(STEP)]))
    if later == WIDTH:
        return
    index = at + (lane % 64) // GROUP
    own = lane % GROUP == iota((GROUP, WIDTH), 0)
    left = []
    for i in range(later, WIDTH):
        value = jnp.take_along_axis(get(i), index, axis=1, mode="promise_in_bounds")
        value = jnp.where(own, value, 0.0)
        high = value.astype(bf16).astype(f32)
        left.append(jnp.where(lane < 64, high, value - high))
    left = jnp.concatenate(left, axis=0).astype(bf16)
    right = jnp.concatenate(split(jnp.concatenate(back, axis=0)), axis=1)
    right = jnp.concatenate([right, right], axis=0)
    out = lax.dot_general(left, right, (((1,), (0,)), ((), ())), preferred_element_type=f32)
    out = out[:, :WIDTH] + out[:, WIDTH:]
    for i in range(later, WIDTH):
        put(i, start(i) - out[GROUP * (i - later) : GROUP * (i - later + 1), :])


def position():
    return lax.axis_index("grp") * lax.axis_size("dev") + lax.axis_index("dev")


def local_kernel(
    counts_in, coords_in, proxies_in, leaf_in, node_in,
    basis_ref, gram_ref, heads_ref, message_ref, move_ref, columns_ref, coords_ref,
    counts, coords, proxies, leaf_t, node_t, sems,
):
    pairs = ((counts_in, counts), (coords_in, coords), (proxies_in, proxies), (leaf_in, leaf_t), (node_in, node_t))
    copies = [pltpu.make_async_copy(a, b, sems.at[i]) for i, (a, b) in enumerate(pairs)]
    for copy in copies:
        copy.start()
    leaves = basis_ref.shape[0]
    eye = unit(ridge)
    shape = (WIDTH, WIDTH)
    for copy in copies[:3]:
        copy.wait()
    grams = []
    lane = iota((1, WIDTH), 1)
    for leaf in range(leaves):
        span = slice(leaf * WIDTH, leaf * WIDTH + WIDTH)
        own = coords[:, span]
        valid = lane < counts[leaf]
        at = WIDTH + 3 * leaf
        message_ref[at : at + 1, :] = jnp.where(valid, own[0:1], -far)
        message_ref[at + 1 : at + 3, :] = own[1:3]
        turned = jnp.concatenate([jnp.where(valid, own[0:1], far), own[1:3], jnp.zeros((5, WIDTH), f32)], axis=0).T
        side = [jnp.broadcast_to(turned[:, d : d + 1], shape) for d in range(3)]
        for d in range(3):
            columns_ref[leaf, d] = side[d]
        basis = matern(*(side[d] - jnp.broadcast_to(proxies[d : d + 1, span], shape) for d in range(3)))
        basis_ref[leaf] = basis
        gram = product(basis, basis, 0, 0) * (1.0 / WIDTH) + eye
        gram_ref[pl.ds(leaf, WIDTH, stride=GROUP), :] = gram
        grams.append(gram)
    copies[3].wait()
    weights = [lift(leaf_t[leaf], grams[leaf]) for leaf in range(leaves)]
    copies[4].wait()
    move_ref[...] = node_t[0]
    heads_ref[pl.ds(GROUP - 1, WIDTH, stride=GROUP), :] = eye
    at = 0
    level = 1
    while len(weights) > 1:
        following = []
        for k in range(len(weights) // 2):
            head = weights[2 * k] + weights[2 * k + 1] + eye
            heads_ref[pl.ds(at, WIDTH, stride=GROUP), :] = head
            at += 1
            following.append(lift(node_t[k * 2**level + 2 ** (level - 1)], head))
        weights = following
        level += 1
    message_ref[0:WIDTH, :] = weights[0]
    coords_ref[...] = message_ref[WIDTH:, :]


def lift_kernel(left, right, move, chosen_in, token, weight_ref, chosen_ref, *, level):
    del token
    span = slice(0, WIDTH)
    head = left[span, :] + right[span, :] + unit(ridge)
    mine = position() % (2 ** (level + 1)) == 2**level
    chosen_ref[...] = jnp.where(mine, head, chosen_in[span, :])
    weight_ref[...] = lift(move[...], head)


def node_slots():
    slots = []
    level = 1
    while 2**level <= GROUP:
        slots += [k * 2**level + 2 ** (level - 1) for k in range(GROUP // 2**level)]
        level += 1
    return slots


class Copies:
    def __init__(self, sems):
        self.sems, self.made = sems, []

    def start(self, source, target):
        copy = pltpu.make_async_copy(source, target, self.sems.at[len(self.made)])
        copy.start()
        self.made.append(copy)

    def wait(self):
        for copy in self.made:
            copy.wait()


def near_tiles(ref, near, flush, copies):
    for n, leaf in enumerate(flush):
        copies.start(ref["tiles_in"].at[n], ref["near_out"].at[leaf])
    if not near:
        return None, 0
    ids, columns, wide = ref["ids"], ref["columns"], ref["wide"]
    leaves, fan = ids.shape[1], ids.shape[0]
    size = ref["swapped"].shape[0]
    odd = position() % 2 == 1
    first, own, second = (ref[n][-size:, :] for n in ("pair", "own", "swapped"))
    wide[0:size, :] = jnp.where(odd, first, second)
    wide[size : 2 * size, :] = own
    wide[2 * size : 3 * size, :] = jnp.where(odd, second, first)
    offset = (position() - 1) * leaves
    total = len(near) * fan
    later = "tiles_out" in ref
    tiles = ref["tiles_out" if later else "tiles"]

    def tile(t):
        at, n = divmod(t, fan)
        leaf = near[at]
        other = wide[pl.ds(3 * (ids[n, leaf] - offset), 3), :]
        shape = (WIDTH, WIDTH)
        value = matern(*(columns[leaf, d] - jnp.broadcast_to(other[d : d + 1], shape) for d in range(3)))
        tiles[at, n] = value.astype(bf16)
        if n == fan - 1 and not later:
            copies.start(tiles.at[at], ref["near_out"].at[leaf])

    return tile, total


def work_kernel(*refs, names, steps, near, flush, final):
    ref = dict(zip(names, refs))
    held = ({}, {})
    copies = Copies(ref["sems"]) if "sems" in ref else None
    tile, total = near_tiles(ref, near, flush, copies)
    done = 0
    share = -(-total // max(1, len(steps) - 1)) if steps else total
    for s in steps:
        for side, name in enumerate(("leaf", "node")):
            source, values = ref[name + "_in"], held[side]
            base = STEP * steps[0]

            def get(i, source=source, values=values):
                return values[i] if i in values else rows_of(source, i)

            def put(i, value, values=values):
                values[i] = value

            def store(kind):
                target = ref[kind]

                def put_row(i, value):
                    target[GROUP * (i - base) : GROUP * (i - base + 1), :] = value

                return put_row

            eliminate(s, get, put, store(name + "_r"), store("leaf_s") if name == "leaf" else None)
            if side == 0:
                for t in range(done, min(done + share, total)):
                    tile(t)
                done += share
    for side, name in enumerate(("leaf", "node")):
        if name + "_out" in ref:
            for i in range(STEP * (steps[-1] + 1), WIDTH):
                ref[name + "_out"][GROUP * i : GROUP * (i + 1), :] = held[side][i]
    if "coords_out" in ref:
        ref["coords_out"][...] = ref["message"][WIDTH:, :]
    if not final:
        if copies:
            copies.wait()
        return
    if not steps:
        for t in range(total):
            tile(t)
    parts = {kind: [ref[f"{kind}{n}"] for n in range(final)] for kind in ("leaf_r", "leaf_s", "node_r")}
    upper = iota((WIDTH, WIDTH), 1) >= iota((WIDTH, WIDTH), 0)
    lower = iota((WIDTH, WIDTH), 1) <= iota((WIDTH, WIDTH), 0)

    def whole(kind, b):
        return jnp.concatenate([stacked(part, b) for part in parts[kind]], axis=0)

    for b in range(GROUP):
        ref["factors"][b] = jnp.where(upper, whole("leaf_r", b), 0.0)
        copies.start(ref["factors"].at[b], ref["leaf_factors"].at[b])
        if b < GROUP - 1:
            ref["nodes"][b] = jnp.where(upper, whole("node_r", b), 0.0)
            copies.start(ref["nodes"].at[b], ref["node_factors"].at[node_slots()[b]])
    for b in range(GROUP):
        span = pl.ds(b * WIDTH, WIDTH)
        turned = jnp.where(lower, whole("leaf_s", b), 0.0)
        ref["bases"][span, :] = product(ref["basis"][b], turned, 1, 1).astype(bf16)
        copies.start(ref["bases"].at[span, :], ref["leaf_bases"].at[span, :])
    copies.wait()


def top_kernel(*refs, names, near, flush, half):
    ref = dict(zip(names, refs))
    copies = Copies(ref["sems"])
    tile, total = near_tiles(ref, near, flush, copies)
    left, right, chosen = ref["left"], ref["right"], ref["chosen"]
    top = jnp.where(position() % half == 0, left[...] + right[...] + unit(ridge), chosen[...])
    values = {}

    def get(i):
        return values[i] if i in values else jnp.broadcast_to(top[i : i + 1, :], (GROUP, WIDTH))

    def put(i, value):
        values[i] = value

    lane = iota((1, WIDTH), 1)
    target = ref["factor"]

    def put_r(i, value):
        target[i : i + 1, :] = jnp.where(lane >= i, value[0:1, :], 0.0)

    share = -(-total // (STEPS - 4))
    for s in range(STEPS):
        eliminate(s, get, put, put_r, None)
        for t in range(s * share, min((s + 1) * share, total)):
            tile(t)
    copies.start(target, ref["node_out"].at[0])
    copies.wait()


def call(body, operands, outs, scratch, aliases, micros, name, **static):
    names = [o[0] for o in operands] + [o[0] for o in outs] + [s[0] for s in scratch]
    at = {o[0]: n for n, o in enumerate(operands)}
    to = {o[0]: n for n, o in enumerate(outs)}
    made = pl.pallas_call(
        functools.partial(body, names=names, **static),
        out_shape=[o[1] for o in outs],
        in_specs=[o[2] for o in operands],
        out_specs=[o[2] for o in outs],
        scratch_shapes=[s[1] for s in scratch],
        input_output_aliases={at[a]: to[b] for a, b in aliases.items()},
        compiler_params=params,
        cost_estimate=cost(micros),
        name=name,
    )(*(o[1] for o in operands))
    return dict(zip(to, made))


def shards(coords, counts, neighbours, proxies, leaf_transfers, node_transfers):
    leaves = counts.shape[0]
    slots = coords.shape[1] // leaves
    fan = neighbours.shape[0]
    count = lax.axis_size("grp") * lax.axis_size("dev")
    levels = count.bit_length() - 1
    half = count // 2
    both = ("grp", "dev")
    shape = jax.ShapeDtypeStruct
    mat = shape((WIDTH, WIDTH), f32)
    mats = shape((leaves, WIDTH, WIDTH), f32)
    flat = shape((WIDTH * GROUP, WIDTH), f32)
    coords_shape = shape((3 * leaves, WIDTH), f32)
    long = shape((WIDTH + 3 * leaves, WIDTH), f32)

    basis, gram, heads, message, move, columns, coords_own = pl.pallas_call(
        local_kernel,
        out_shape=(mats, flat, flat, long, mat, shape((leaves, 3, slots, WIDTH), f32), coords_shape),
        in_specs=[anywhere] * 5,
        out_specs=(vmem,) * 7,
        scratch_shapes=[
            pltpu.SMEM(counts.shape, jnp.int32),
            pltpu.VMEM(coords.shape, f32),
            pltpu.VMEM(proxies.shape, f32),
            pltpu.VMEM(leaf_transfers.shape, f32),
            pltpu.VMEM(node_transfers.shape, f32),
            pltpu.SemaphoreType.DMA((5,)),
        ],
        compiler_params=params,
        cost_estimate=cost(4),
        name="local",
    )(*(pltpu.with_memory_space_constraint(x, pltpu.HBM) for x in (counts, coords, proxies, leaf_transfers, node_transfers)))

    plan = [
        ((0, 1, 2, 3, 4), ()),
        ((5, 6, 7), ()),
        ((8, 9, 10), ()),
        ((11, 12, 13, 14, 15), (0, 1, 2)),
        ((), (3, 4, 5)),
    ]
    parts = []
    last_near = tuple(range(6, leaves))
    state = dict(leaf=gram, node=heads, near=None, tiles=None, flush=())

    def near_extras(near, flush, later, operands, outs, scratch, aliases):
        if near:
            operands += [("ids", neighbours, smem), ("own", message, vmem), ("pair", pair, vmem)]
            operands += [("swapped", swapped, vmem), ("columns", columns, vmem)]
            scratch.append(("wide", pltpu.VMEM((9 * leaves, WIDTH), f32)))
            tiles = (len(near), fan, slots, slots)
            if later:
                outs.append(("tiles_out", shape(tiles, bf16), vmem))
            else:
                scratch.append(("tiles", pltpu.VMEM(tiles, bf16)))
        if flush:
            operands.append(("tiles_in", state["tiles"], vmem))
        if flush or (near and not later):
            outs.append(("near_out", shape((leaves, fan, slots, slots), bf16), anywhere))
            if state["near"] is not None:
                operands.append(("near_in", state["near"], anywhere))
                aliases["near_in"] = "near_out"

    def work(n, after):
        steps, near = plan[n]
        aliases = {}
        final = n == len(plan) - 1
        operands = [("after", after, anywhere)]
        outs, scratch = [], []
        if steps:
            rows = shape((STEP * len(steps) * GROUP, WIDTH), f32)
            operands += [("leaf_in", state["leaf"], vmem), ("node_in", state["node"], vmem)]
            outs += [(kind, rows, vmem) for kind in ("leaf_r", "leaf_s", "node_r")]
            if steps[-1] + 1 < STEPS:
                outs += [("leaf_out", flat, vmem), ("node_out", flat, vmem)]
        flush = state["flush"]
        near_extras(near, flush, True, operands, outs, scratch, aliases)
        if final:
            for k, part in enumerate(parts):
                operands += [(f"{kind}{k}", part[kind], vmem) for kind in ("leaf_r", "leaf_s", "node_r")]
            operands.append(("basis", basis, vmem))
            outs += [("leaf_factors", mats, anywhere), ("node_factors", mats, anywhere)]
            outs.append(("leaf_bases", shape((leaves * slots, WIDTH), bf16), anywhere))
            scratch += [("factors", pltpu.VMEM(mats.shape, f32)), ("nodes", pltpu.VMEM(mats.shape, f32))]
            scratch.append(("bases", pltpu.VMEM((leaves * slots, WIDTH), bf16)))
        if flush or final:
            scratch.append(("sems", pltpu.SemaphoreType.DMA((3 * GROUP + leaves,))))
        made = call(
            work_kernel, operands, outs, scratch, aliases, 3, f"work{n}",
            steps=steps, near=near, flush=flush, final=len(parts) if final else 0,
        )
        state["near"] = made.get("near_out", state["near"])
        state["tiles"], state["flush"] = made.get("tiles_out"), near
        if steps:
            parts.append(made)
            state["leaf"], state["node"] = made.get("leaf_out"), made.get("node_out")
        return made

    weight = chosen = message
    made = pair = None
    others = [(i, i + 1) for i in range(1, count - 1, 2)]
    others += [(target, source) for source, target in others]
    swapped = lax.ppermute(coords_own, both, others)
    for level in range(levels):
        span = 2 ** (level + 1)
        quarter = span // 4
        if level == 0:
            pair = lax.ppermute(weight, both, [(i, i ^ 1) for i in range(count)])
            left, right = pair, weight
        else:
            first = [(i + quarter, i + 2 * quarter) for i in range(0, count, span)]
            second = [(i + 3 * quarter, i + 2 * quarter) for i in range(0, count, span)]
            if level + 1 == levels:
                first.append((3 * quarter, 0))
                second.append((quarter, 0))
            left, right = lax.ppermute(weight, both, first), lax.ppermute(weight, both, second)
        if level < len(plan):
            made = work(level, weight)
        if level + 1 < levels:
            weight, chosen = pl.pallas_call(
                functools.partial(lift_kernel, level=level),
                out_shape=[mat, mat],
                in_specs=[vmem] * 4 + [anywhere],
                out_specs=[vmem] * 2,
                compiler_params=params,
                cost_estimate=cost(0.4),
                name=f"lift{level}",
            )(left, right, move, chosen, next(iter(made.values())))

    operands = [
        ("left", left, vmem), ("right", right, vmem), ("chosen", chosen, vmem),
        ("node_in", made["node_factors"], anywhere),
    ]
    outs = [("node_out", mats, anywhere)]
    scratch = [("factor", pltpu.VMEM((WIDTH, WIDTH), f32)), ("sems", pltpu.SemaphoreType.DMA((leaves + 1,)))]
    aliases = {"node_in": "node_out"}
    near_extras(last_near, state["flush"], False, operands, outs, scratch, aliases)
    top = call(
        top_kernel, operands, outs, scratch, aliases, 6, "top", near=last_near, flush=state["flush"], half=half
    )
    return (top["near_out"], made["leaf_bases"], made["leaf_factors"], top["node_out"])


def solution(mesh):
    both = ("grp", "dev")
    in_specs = (
        P(None, both),
        P(both),
        P(None, both),
        P(None, both),
        P(both, None, None),
        P(both, None, None),
    )
    out_specs = (
        P(both, None, None, None),
        P(both, None),
        P(both, None, None),
        P(both, None, None),
    )
    return jax.shard_map(shards, mesh=mesh, in_specs=in_specs, out_specs=out_specs, check_vma=False)
```
